32 devices in a mesh: section: 2 (over x), fsdp: 16 (over z, y, core).
Axes of the slice: x: 2, y: 2, z: 4, core: 2. Of those that a mesh axis runs over, the one named last changes fastest.
Arguments:
- fwd_prev: bfloat16 [2, 1024, 4608], P('section', 'fsdp'), may hold values from -6 to 6
- saved: bfloat16 [2, 1024, 4608], P('section', 'fsdp'), may hold values from -6 to 6
- back_prev: bfloat16 [2, 1024, 4608], P('section', 'fsdp'), may hold values from -6 to 6
- fwd_docs: int32 [2, 1024], P('section', 'fsdp'), may hold values from 0 to 31, never falling along the last dimension, each value on 1 to 64 neighbouring positions
- back_docs: int32 [2, 1024], P('section', 'fsdp'), may hold values from 0 to 31, never falling along the last dimension, each value on 1 to 64 neighbouring positions
- gain: float32 [2, 4608], P('section'), may hold values from 0.5 to 1.5
- weight: bfloat16 [2, 4608, 768], P('section', 'fsdp'), may hold values from -0.09375 to 0.09375
Outputs:
- fwd_out: bfloat16 [2, 1024, 4608], P('section', 'fsdp')
- back_out: bfloat16 [2, 1024, 4608], P('section', 'fsdp')
The draws below stay inside these ranges and needn't reach their ends.
Inputs may be any that keep to these rules, and one draw needn't show every extreme that they name: fwd_docs never falls along the rows of a section; a document spans 1 to 64 rows. back_docs never falls along the rows of a section; a document spans 1 to 64 rows.
All inputs are finite; a program needn't handle non-finite values.
Results may differ from the reference program's by a relative error of at most 0.011.
Values may be sent and summed in bfloat16 or wider, within the bound.
No kernel may reach another device: no remote copies, remote signals or barrier semaphores. Data moves between devices by JAX's collectives and lax.ppermute only.
A program may use at most 64 MiB of HBM per device.

```python
import math
import jax
import jax.numpy as jnp
import numpy as np
from jax import lax

D = 4608
HD = 96
KVH = 4
GROUP = 12
KVC = 768
ROWS = 64
ROWS_ALL = 1024
N_SECTION = 2


def shard_levels(key, dims, split, least, top_value):
    def one(dim, blocks):
        heights = jax.random.uniform(jax.random.fold_in(jax.random.fold_in(key, 6), dim), (blocks,), jnp.float32, least / len(split), top_value / len(split))
        return jnp.repeat(jnp.exp(heights), dims[dim] // blocks).reshape((-1,) + (1,) * (len(dims) - dim - 1))

    factor_of = one(*split[0])
    for cut in split[1:]:
        factor_of = factor_of * one(*cut)
    return factor_of


def split_up(amount, total, reach, slope):
    weights = [(1 << 20) // math.isqrt(grade ** slope) + 1 for grade in range(2, amount + 1)]
    surplus, given = total - reach - (amount - 1), [1] * (amount - 1)
    while surplus > 0:
        movable = [i for i in range(amount - 1) if given[i] < reach]
        mass, left = sum([weights[i] for i in movable]), surplus
        for i in movable:
            extra = min(reach - given[i], max(1, left * weights[i] // mass), surplus)
            given[i] = given[i] + extra
            surplus = surplus - extra
    return np.array([reach] + given)


def ragged(rng, count, total, bound, lean):
    if count == 2:
        one = jax.random.randint(rng, (), max(1, total - bound), min(bound, total - 1) + 1)
        return jnp.stack([one, total - one])
    sizes = jnp.asarray(split_up(count, total, bound, lean), jnp.int32)
    pairs = (count - 1) // 2
    donor, sink = sizes[1:1 + 2 * pairs:2], sizes[2:2 + 2 * pairs:2]
    slack = jnp.minimum(donor - 1, bound - sink)
    passed = jax.random.randint(jax.random.fold_in(rng, 1), (pairs,), 0, 1 << 20) % (slack + 1)
    sizes = sizes.at[1:1 + 2 * pairs:2].set(donor - passed).at[2:2 + 2 * pairs:2].set(sink + passed)
    return sizes[jax.random.permutation(jax.random.fold_in(rng, 2), count)]


def centred(stream_key, dims, width, bound, split=(), dtype=jnp.bfloat16):
    level = shard_levels(stream_key, dims, split, -0.22, 0.18) if split else 1.0
    values = jax.random.normal(stream_key, dims, jnp.float32) * width * level
    return jnp.minimum(jnp.maximum(values, -bound), bound).astype(dtype)


def setup_inputs(seed: int = 0) -> dict:
    arg_keys = jax.random.split(jax.random.key(seed), 8)
    fwd_prev = centred(arg_keys[0], (N_SECTION, ROWS_ALL, D), 1.0, 6.0, ((0, 2), (1, 16)))
    saved = centred(arg_keys[1], (N_SECTION, ROWS_ALL, D), 1.0, 6.0, ((0, 2), (1, 16)))
    back_prev = centred(arg_keys[2], (N_SECTION, ROWS_ALL, D), 1.0, 6.0, ((0, 2), (1, 16)))
    fwd_docs = jax.vmap(lambda own: jnp.searchsorted(jnp.cumsum(ragged(own, ROWS_ALL // 32, ROWS_ALL, 64, 2)), jnp.arange(ROWS_ALL), side="right"))(jax.random.split(arg_keys[3], N_SECTION)).reshape((N_SECTION, ROWS_ALL)).astype(jnp.int32)
    back_docs = jax.vmap(lambda own: jnp.searchsorted(jnp.cumsum(ragged(own, ROWS_ALL // 32, ROWS_ALL, 64, 2)), jnp.arange(ROWS_ALL), side="right"))(jax.random.split(arg_keys[4], N_SECTION)).reshape((N_SECTION, ROWS_ALL)).astype(jnp.int32)
    gain = jnp.clip(1.0 + 0.1 * jax.random.normal(arg_keys[5], (N_SECTION, D), jnp.float32), 0.5, 1.5)
    weight = centred(arg_keys[6], (N_SECTION, D, KVC), D ** -0.5, 0.09375, ((0, 2), (1, 16)))
    return {"fwd_prev": fwd_prev, "saved": saved, "back_prev": back_prev, "fwd_docs": fwd_docs, "back_docs": back_docs, "gain": gain, "weight": weight}


EPSILON = 1e-05

def normed(rows_in, gain_row):
    values = rows_in.astype(jnp.float32)
    mean_square = lax.optimization_barrier(jnp.mean(values * values, axis=-1, keepdims=True))
    return (values * lax.rsqrt(mean_square + EPSILON) * gain_row).astype(jnp.bfloat16)

def attend(rows_in, hidden, keyval, doc_ids):
    row_count = rows_in.shape[0]
    queries = hidden.astype(jnp.float32).reshape(row_count, KVH, GROUP, HD)
    key_rows = keyval[:, :KVH * HD].astype(jnp.float32).reshape(row_count, KVH, HD)
    value_rows = keyval[:, KVH * HD:].astype(jnp.float32).reshape(row_count, KVH, HD)
    scores = jnp.einsum('ikgd,jkd->kgij', queries, key_rows) * HD ** (-0.5)
    position = jnp.arange(row_count)
    allowed = (doc_ids[:, None] == doc_ids[None, :]) & (position[None, :] <= position[:, None])
    scores = jnp.where(allowed, scores, -1e+30)
    probs = jax.nn.softmax(scores, axis=-1).astype(jnp.bfloat16)
    mixed_rows = jnp.einsum('kgij,jkd->ikgd', probs.astype(jnp.float32), value_rows)
    return (rows_in.astype(jnp.float32) + mixed_rows.reshape(row_count, D)).astype(jnp.bfloat16)

def block_attend(rows_in, hidden, keyval, doc_ids):
    outcome = jax.vmap(attend)(rows_in.reshape(-1, ROWS, D), hidden.reshape(-1, ROWS, D), keyval.reshape(-1, ROWS, KVC), doc_ids.reshape(-1, ROWS))
    return outcome.reshape(-1, D)

def forward_rows(rows_in, doc_ids, gain_row, weight_full):
    hidden = normed(rows_in, gain_row)
    keyval = jnp.dot(hidden, weight_full, preferred_element_type=jnp.float32).astype(jnp.bfloat16)
    return block_attend(rows_in, hidden, keyval, doc_ids)

def backward_rows(saved_rows, doc_ids, cotangent, gain_row, weight_full):
    hidden, norm_back = jax.vjp(lambda rows_in: normed(rows_in, gain_row), saved_rows)
    keyval = jnp.dot(hidden, weight_full, preferred_element_type=jnp.float32).astype(jnp.bfloat16)
    outcome, attend_back = jax.vjp(lambda rows_in, hidden_in, keyval_in: block_attend(rows_in, hidden_in, keyval_in, doc_ids), saved_rows, hidden, keyval)
    grad_rows, grad_hidden, grad_keyval = attend_back(cotangent)
    through = (grad_hidden.astype(jnp.float32) + jnp.dot(grad_keyval, weight_full.T, preferred_element_type=jnp.float32)).astype(jnp.bfloat16)
    grad_norm = norm_back(through)[0]
    return (grad_rows.astype(jnp.float32) + grad_norm.astype(jnp.float32)).astype(jnp.bfloat16)

def reference(fwd_prev, saved, back_prev, fwd_docs, back_docs, gain, weight):
    incoming = jnp.roll(fwd_prev, 1, axis=0)
    cotangent = jnp.roll(back_prev, -1, axis=0)

    def one_section(section_items):
        rows_in, saved_rows, section_cot, docs_fwd, docs_back, gain_row, weight_full = section_items
        return (forward_rows(rows_in, docs_fwd, gain_row, weight_full), backward_rows(saved_rows, docs_back, section_cot, gain_row, weight_full))
    fwd_out, back_out = lax.map(one_section, (incoming, saved, cotangent, fwd_docs, back_docs, gain, weight))
    return (fwd_out, back_out)
```

```python
import functools

import jax
import jax.numpy as jnp
from jax import lax
from jax.experimental import pallas as pl
from jax.experimental.pallas import tpu as pltpu
from jax.sharding import PartitionSpec as P

HD = 96
KVH = 4
GROUP = 12
ROWS = 64
SIDE = 4
EPSILON = 1e-05

F32 = jnp.float32
BF16 = jnp.bfloat16


def dot(a, b, over=((1,), (0,))):
    return lax.dot_general(a, b, (over, ((), ())), preferred_element_type=F32)


def norm_kernel(u_ref, gain_ref, hidden_ref, cut_ref, scale_ref):
    rows, width = u_ref.shape
    pieces, _, depth = cut_ref.shape
    step = width // 9
    total = jnp.zeros((rows, 1), F32)
    for c in range(0, width, step):
        values = u_ref[:, c : c + step].astype(F32)
        total = total + jnp.sum(values * values, axis=-1, keepdims=True)
    scale = lax.rsqrt(total / width + EPSILON)
    scale_ref[...] = jnp.broadcast_to(scale, scale_ref.shape)
    for c in range(0, width, step):
        values = u_ref[:, c : c + step].astype(F32)
        hidden_ref[:, c : c + step] = (values * scale * gain_ref[:, c : c + step]).astype(BF16)
    for p in range(pieces):
        cut_ref[p] = hidden_ref[:, p * depth : (p + 1) * depth]


def norm_call(rows_in, gain, pieces):
    rows, width = rows_in.shape
    return pl.pallas_call(
        norm_kernel,
        out_shape=(
            jax.ShapeDtypeStruct((rows, width), BF16),
            jax.ShapeDtypeStruct((pieces, rows, width // pieces), BF16),
            jax.ShapeDtypeStruct((rows, 128), F32),
        ),
        cost_estimate=pl.CostEstimate(
            flops=6 * rows * width, bytes_accessed=6 * rows * width, transcendentals=rows
        ),
        name="norm",
    )(rows_in, gain)


def piece_index(offset, factors, axis):
    me = 0 if axis is None else lax.axis_index(axis)
    index, stride = 0, 1
    for size, away in zip(reversed(factors), reversed(offset)):
        index = index + lax.rem(lax.rem(lax.div(me, stride), size) + away, size) * stride
        stride = stride * size
    return index


def keyval_kernel(offsets, factors, axis, with_total, *refs):
    cut_f, cut_b = refs[:2]
    weights, refs = refs[2 : 2 + len(offsets)], refs[2 + len(offsets) :]
    total = refs[0][...] if with_total else None
    for offset, weight in zip(offsets, weights):
        at = piece_index(offset, factors, axis)
        part = dot(jnp.concatenate([cut_f[at], cut_b[at]], axis=0), weight[...])
        total = part if total is None else total + part
    refs[-1][...] = total


def keyval_call(cut_f, cut_b, weights, offsets, factors, axis, total):
    rows, columns = 2 * cut_f.shape[1], weights[0].shape[1]
    work = rows * columns * sum(w.shape[0] for w in weights)
    return pl.pallas_call(
        functools.partial(keyval_kernel, offsets, factors, axis, total is not None),
        out_shape=jax.ShapeDtypeStruct((rows, columns), F32),
        cost_estimate=pl.CostEstimate(
            flops=2 * work, bytes_accessed=work // rows * 2, transcendentals=0
        ),
        name="keyval",
    )(cut_f, cut_b, *weights, *(() if total is None else (total,)))


def beside(x):
    rows, width = x.shape
    wide = jnp.concatenate([x] * SIDE, axis=1)
    lane = lax.broadcasted_iota(jnp.int32, wide.shape, 1)
    blocks = [
        jnp.where((lane >= j * width) & (lane < (j + 1) * width), wide, jnp.zeros_like(wide))
        for j in range(SIDE)
    ]
    return jnp.concatenate(blocks, axis=0)


def diagonal(x, rows, width):
    total = x[:rows, :width]
    for j in range(1, SIDE):
        total = total + x[j * rows : (j + 1) * rows, j * width : (j + 1) * width]
    return total


def same_segment(rows):
    size = SIDE * rows
    a = lax.broadcasted_iota(jnp.int32, (size, size), 0) // rows
    b = lax.broadcasted_iota(jnp.int32, (size, size), 1) // rows
    return (a == b).astype(F32).astype(BF16)


def segment_sum(x, ones):
    high = x.astype(BF16)
    low = (x - high.astype(F32)).astype(BF16)
    return dot(high, ones) + dot(low, ones)


def segment_max(x, rows):
    size = x.shape[1]
    lane = lax.broadcasted_iota(jnp.int32, x.shape, 1)
    result = None
    for j in range(SIDE):
        inside = (lane >= j * rows) & (lane < (j + 1) * rows)
        top = jnp.max(jnp.where(inside, x, -3e38), axis=-1, keepdims=True)
        result = top + jnp.zeros_like(x) if result is None else jnp.where(lane >= j * rows, top, result)
    return result


def probabilities(queries, keys, allowed, ones, rows):
    scores = dot(queries, keys, ((1,), (1,))) * HD**-0.5
    scores = jnp.where(allowed, scores, -1e30)
    powers = jnp.exp(scores - segment_max(scores, rows))
    return powers / segment_sum(powers, ones)


def allowed_mask(docs_col, docs_row):
    rows, size = docs_col.shape[0], docs_row.shape[1]
    shape = (rows, size)
    row = lax.broadcasted_iota(jnp.int32, shape, 0)
    col = lax.rem(lax.broadcasted_iota(jnp.int32, shape, 1), rows)
    allowed = ((docs_col[...] == docs_row[...]) & (col <= row)).astype(F32)
    return jnp.concatenate([allowed] * (GROUP // SIDE), axis=0) > 0.5


def stacked(ref, k):
    wide = SIDE * HD
    groups = GROUP // SIDE
    return jnp.concatenate(
        [ref[:, (k * groups + g) * wide : (k * groups + g + 1) * wide] for g in range(groups)], axis=0
    )


def tail_kernel(offsets, last, factors, axis, *refs):
    n = len(offsets)
    (total_ref, hid_f, hid_b, cut_f, cut_b, u_ref, saved_ref, cot_ref, gain_ref, scale_ref,
     col_f, row_f, col_b, row_b), refs = refs[:14], refs[14:]
    pieces, refs = refs[:n], refs[n:]
    fwd_ref, back_ref, weight, grad_kv, grad_q, sems = refs
    depth = pieces[0].shape[0]
    rows, width = u_ref.shape
    keys = KVH * HD
    groups = GROUP // SIDE
    wide = SIDE * HD

    copies, places = [], []
    for i in range(n):
        at = piece_index(offsets[i], factors, axis)
        place = pl.ds(pl.multiple_of(at * depth, 16), depth)
        copies.append(pltpu.make_async_copy(pieces[i], weight.at[place, :], sems.at[i]))
        places.append((at, place))
    for i in (*range(n - last, n), *range(n - last)):
        copies[i].start()
    total = total_ref[...]
    for i in range(n - last, n):
        copies[i].wait()
        at, place = places[i]
        total = total + dot(jnp.concatenate([cut_f[at], cut_b[at]], axis=0), weight[place, :])
    keyval = total.astype(BF16)
    ones = same_segment(rows)
    mask_f = allowed_mask(col_f, row_f)
    mask_b = allowed_mask(col_b, row_b)
    for k in range(KVH):
        key = beside(keyval[rows:, k * HD : (k + 1) * HD])
        value = beside(keyval[rows:, keys + k * HD : keys + (k + 1) * HD])
        queries, grads = stacked(hid_b, k), stacked(cot_ref, k)
        probs = probabilities(queries, key, mask_b, ones, rows)
        grad_probs = dot(grads, value, ((1,), (1,))).astype(BF16).astype(F32)
        mean = segment_sum(probs * grad_probs, ones)
        grad_scores = (probs * (grad_probs - mean) * HD**-0.5).astype(BF16)
        grad_queries = dot(grad_scores, key).astype(BF16)
        for g in range(groups):
            at = (k * groups + g) * wide
            grad_q[:, at : at + wide] = grad_queries[g * rows : (g + 1) * rows]
        grad_key = diagonal(dot(grad_scores, queries, ((0,), (0,))), rows, HD)
        grad_value = diagonal(dot(probs.astype(BF16), grads, ((0,), (0,))), rows, HD)
        grad_kv[:, k * HD : (k + 1) * HD] = grad_key.astype(BF16)
        grad_kv[:, keys + k * HD : keys + (k + 1) * HD] = grad_value.astype(BF16)
    for k in range(KVH):
        key = beside(keyval[:rows, k * HD : (k + 1) * HD])
        value = beside(keyval[:rows, keys + k * HD : keys + (k + 1) * HD])
        probs = probabilities(stacked(hid_f, k), key, mask_f, ones, rows)
        mixed = dot(probs.astype(BF16), value)
        for g in range(groups):
            at = (k * groups + g) * wide
            fwd_ref[:, at : at + wide] = (
                u_ref[:, at : at + wide].astype(F32) + mixed[g * rows : (g + 1) * rows]
            ).astype(BF16)
    for i in range(n - last):
        copies[i].wait()
    grads = grad_kv[...]
    step = width // 9
    along = jnp.zeros((rows, 1), F32)
    for c in range(0, width, step):
        at = slice(c, c + step)
        through = dot(grads, weight[at, :], ((1,), (1,))) + grad_q[:, at].astype(F32)
        through = through.astype(BF16)
        grad_q[:, at] = through
        part = through.astype(F32) * gain_ref[:, at] * saved_ref[:, at].astype(F32)
        along = along + jnp.sum(part, axis=-1, keepdims=True)
    scale = scale_ref[:, :1]
    along = along * (scale * scale * scale) / width
    for c in range(0, width, step):
        at = slice(c, c + step)
        grad = grad_q[:, at].astype(F32) * gain_ref[:, at] * scale
        grad = (grad - saved_ref[:, at].astype(F32) * along).astype(BF16)
        back_ref[:, at] = (cot_ref[:, at].astype(F32) + grad.astype(F32)).astype(BF16)


def tail_call(total, hid_f, hid_b, cut_f, cut_b, incoming, saved, cotangent, gain, scale_b,
              docs, pieces, offsets, last, factors, axis):
    rows, width = incoming.shape
    columns = total.shape[1]
    n = len(pieces)
    vmem = pl.BlockSpec(memory_space=pltpu.VMEM)
    return pl.pallas_call(
        functools.partial(tail_kernel, offsets, last, factors, axis),
        out_shape=(jax.ShapeDtypeStruct((rows, width), BF16),) * 2,
        in_specs=[vmem] * 14 + [pl.BlockSpec(memory_space=pl.ANY)] * n,
        out_specs=(vmem, vmem),
        scratch_shapes=[
            pltpu.VMEM((width, columns), BF16),
            pltpu.VMEM((rows, columns), BF16),
            pltpu.VMEM((rows, width), BF16),
            pltpu.SemaphoreType.DMA((n,)),
        ],
        cost_estimate=pl.CostEstimate(
            flops=2 * rows * width * columns, bytes_accessed=2 * width * columns, transcendentals=0
        ),
        name="tail",
    )(total, hid_f, hid_b, cut_f, cut_b, incoming, saved, cotangent, gain, scale_b, *docs, *pieces)


def shifted(x, axis, factors, steps):
    n = lax.axis_size(axis)
    pairs = []
    for me in range(n):
        source, stride = 0, 1
        for size, step in zip(reversed(factors), reversed(steps)):
            source = source + (me // stride % size + step) % size * stride
            stride = stride * size
        pairs.append((source, me))
    return lax.ppermute(x, axis, pairs)


def grid_factors(mesh, axis):
    n = mesh.shape[axis]
    place = list(mesh.axis_names).index(axis)
    devices = mesh.devices
    line = devices[tuple(slice(None) if i == place else 0 for i in range(devices.ndim))]
    spots = [(*getattr(d, "coords", (i,)), getattr(d, "core_on_chip", 0)) for i, d in enumerate(line)]
    factors, stride = [], 1
    while stride < n:
        moved = [i for i in range(len(spots[0])) if spots[stride][i] != spots[0][i]][0]
        size = len({s[moved] for s in spots[::stride]})
        factors.insert(0, size)
        stride *= size
    return tuple(factors)


def on_device(factors, fwd_prev, saved, back_prev, fwd_docs, back_docs, gain, weight):
    sections = lax.axis_size("section")
    n = lax.axis_size("fsdp")
    own = weight[0]
    rows = saved.shape[1]
    ring = lambda x, by: lax.ppermute(x, "section", [(i, (i + by) % sections) for i in range(sections)])
    move = lambda x, *steps: shifted(x, "fsdp", factors, steps)

    if n <= 16 and len(factors) == 3 and factors[0] == 4 and factors[1] == 2 and factors[2] == 2:
        y0 = move(own, 0, 1, 0)
        z1 = move(own, 1, 0, 0)
        z3 = move(own, 3, 0, 0)
        incoming = ring(fwd_prev[0], 1)
        cotangent = ring(back_prev[0], -1)
        c0 = move(own, 0, 0, 1)
        z2 = move(z1, 1, 0, 0)
        y1 = move(z1, 0, 1, 0)
        y3 = move(z3, 0, 1, 0)
        y2 = move(z2, 0, 1, 0)
        across = lambda x: move(x, 0, 0, 1)
        groups = [
            [(own, (0, 0, 0)), (c0, (0, 0, 1)), (y0, (0, 1, 0)), (across(y0), (0, 1, 1)),
             (z1, (1, 0, 0)), (across(z1), (1, 0, 1))],
            [(z3, (3, 0, 0)), (across(z3), (3, 0, 1)), (y1, (1, 1, 0)), (across(y1), (1, 1, 1))],
            [(z2, (2, 0, 0)), (across(z2), (2, 0, 1)), (y3, (3, 1, 0)), (across(y3), (3, 1, 1))],
            [(y2, (2, 1, 0)), (across(y2), (2, 1, 1))],
        ]
        shape = factors
    else:
        incoming = ring(fwd_prev[0], 1)
        cotangent = ring(back_prev[0], -1)
        full = lax.all_gather(own, "fsdp", axis=0, tiled=True)
        half = full.shape[0] // 2
        groups = [[(full[:half], (0,))], [(full[half:], (1,))]]
        shape = (2,)
    pieces = sum(len(g) for g in groups)
    axis = "fsdp"
    if shape != factors:
        axis = None
    hid_b, cut_b, scale_b = norm_call(saved[0], gain, pieces)
    hid_f, cut_f, _ = norm_call(incoming, gain, pieces)
    total = None
    for group in groups[:-1]:
        total = keyval_call(cut_f, cut_b, [w for w, _ in group], [o for _, o in group], shape, axis, total)
    docs = []
    for ids in (fwd_docs[0], back_docs[0]):
        docs += [ids[:, None], jnp.tile(ids, SIDE)[None]]
    every = [piece for group in groups for piece in group]
    fwd_out, back_out = tail_call(
        total, hid_f, hid_b, cut_f, cut_b, incoming, saved[0], cotangent, gain, scale_b, docs,
        [w for w, _ in every], [o for _, o in every], len(groups[-1]), shape, axis,
    )
    return (fwd_out[None], back_out[None])


def solution(mesh):
    in_specs = (
        P("section", "fsdp", None),
        P("section", "fsdp", None),
        P("section", "fsdp", None),
        P("section", "fsdp"),
        P("section", "fsdp"),
        P("section", None),
        P("section", "fsdp", None),
    )
    out_specs = (P("section", "fsdp", None), P("section", "fsdp", None))
    return jax.shard_map(
        functools.partial(on_device, grid_factors(mesh, "fsdp")),
        mesh=mesh, in_specs=in_specs, out_specs=out_specs, check_vma=False,
    )
```

```python
import functools

import jax
import jax.numpy as jnp
from jax import lax
from jax.experimental import pallas as pl
from jax.experimental.pallas import tpu as pltpu
from jax.sharding import PartitionSpec as P


HD = 96
KVH = 4
GROUP = 12
SIDE = 4
EPSILON = 1e-05

F32 = jnp.float32
BF16 = jnp.bfloat16


def dot(a, b, over=((1,), (0,))):
    return lax.dot_general(a, b, (over, ((), ())), preferred_element_type=F32)


def norm_kernel(u_ref, gain_ref, hidden_ref, cut_ref, scale_ref):
    rows, width = u_ref.shape
    pieces, _, depth = cut_ref.shape
    step = width // 9
    total = jnp.zeros((rows, 1), F32)
    for c in range(0, width, step):
        values = u_ref[:, c : c + step].astype(F32)
        total = total + jnp.sum(values * values, axis=-1, keepdims=True)
    scale = lax.rsqrt(total / width + EPSILON)
    scale_ref[...] = jnp.broadcast_to(scale, scale_ref.shape)
    for c in range(0, width, step):
        values = u_ref[:, c : c + step].astype(F32)
        hidden_ref[:, c : c + step] = (values * scale * gain_ref[:, c : c + step]).astype(BF16)
    for p in range(pieces):
        cut_ref[p] = hidden_ref[:, p * depth : (p + 1) * depth]


def norm_call(rows_in, gain, pieces):
    rows, width = rows_in.shape
    return pl.pallas_call(
        norm_kernel,
        out_shape=(
            jax.ShapeDtypeStruct((rows, width), BF16),
            jax.ShapeDtypeStruct((pieces, rows, width // pieces), BF16),
            jax.ShapeDtypeStruct((rows, 128), F32),
        ),
        cost_estimate=pl.CostEstimate(
            flops=6 * rows * width, bytes_accessed=6 * rows * width, transcendentals=rows
        ),
        compiler_params=pltpu.CompilerParams(vmem_limit_bytes=6 << 20),
        name="norm",
    )(rows_in, gain)


def piece_index(offset, factors, axis):
    me = 0 if axis is None else lax.axis_index(axis)
    index, stride = 0, 1
    for size, away in zip(reversed(factors), reversed(offset)):
        index = index + lax.rem(lax.rem(lax.div(me, stride), size) + away, size) * stride
        stride = stride * size
    return index


def add_pieces(places, factors, axis, cut_f, cut_b, pieces, total, weight):
    for (offset, column), piece in zip(places, pieces):
        at = piece_index(offset, factors, axis)
        depth, width = piece.shape
        value = piece[...]
        part = dot(jnp.concatenate([cut_f[at], cut_b[at]], axis=0), value)
        total[:, column : column + width] += part
        weight[pl.ds(pl.multiple_of(at * depth, 16), depth), column : column + width] = value


def keyval_kernel(places, factors, axis, first, *refs):
    cut_f, cut_b = refs[:2]
    pieces, (total, weight) = refs[2 : 2 + len(places)], refs[-2:]
    if first:
        total[...] = jnp.zeros_like(total)
    else:
        old = refs[2 + len(places)]
        total[...] = old[...]
    add_pieces(places, factors, axis, cut_f, cut_b, pieces, total, weight)


def keyval_call(cut_f, cut_b, group, factors, axis, state, shape):
    pieces, places = [p for p, _, _ in group], [(o, c) for _, o, c in group]
    rows = 2 * cut_f.shape[1]
    work = rows * sum(p.size for p in pieces)
    n = 2 + len(pieces)
    return pl.pallas_call(
        functools.partial(keyval_kernel, places, factors, axis, state is None),
        out_shape=(
            jax.ShapeDtypeStruct((rows, shape[1]), F32),
            jax.ShapeDtypeStruct(shape, BF16),
        ),
        input_output_aliases={} if state is None else {n: 0, n + 1: 1},
        cost_estimate=pl.CostEstimate(
            flops=2 * work, bytes_accessed=work // rows * 2, transcendentals=0
        ),
        compiler_params=pltpu.CompilerParams(vmem_limit_bytes=20 << 20),
        name="keyval",
    )(cut_f, cut_b, *pieces, *(() if state is None else state))


def beside(x):
    _, width = x.shape
    wide = jnp.concatenate([x] * SIDE, axis=1)
    lane = lax.broadcasted_iota(jnp.int32, wide.shape, 1)
    blocks = [
        jnp.where((lane >= j * width) & (lane < (j + 1) * width), wide, jnp.zeros_like(wide))
        for j in range(SIDE)
    ]
    return jnp.concatenate(blocks, axis=0)


def diagonal(x, rows, width):
    total = x[:rows, :width]
    for j in range(1, SIDE):
        total = total + x[j * rows : (j + 1) * rows, j * width : (j + 1) * width]
    return total


def same_segment(rows):
    size = SIDE * rows
    a = lax.broadcasted_iota(jnp.int32, (size, size), 0) // rows
    b = lax.broadcasted_iota(jnp.int32, (size, size), 1) // rows
    return (a == b).astype(F32).astype(BF16)


def segment_sum(x, ones):
    high = x.astype(BF16)
    low = (x - high.astype(F32)).astype(BF16)
    return dot(high, ones) + dot(low, ones)


def segment_max(x, rows):
    lane = lax.broadcasted_iota(jnp.int32, x.shape, 1)
    result = None
    for j in range(SIDE):
        inside = (lane >= j * rows) & (lane < (j + 1) * rows)
        top = jnp.max(jnp.where(inside, x, -3e38), axis=-1, keepdims=True)
        result = top + jnp.zeros_like(x) if result is None else jnp.where(lane >= j * rows, top, result)
    return result


def probabilities(queries, keys, allowed, ones, rows):
    scores = dot(queries, keys, ((1,), (1,))) * HD**-0.5
    scores = jnp.where(allowed, scores, -1e30)
    powers = jnp.exp(scores - segment_max(scores, rows))
    return powers / segment_sum(powers, ones)


def allowed_mask(docs_ref):
    rows = docs_ref.shape[1]
    row = lax.broadcasted_iota(jnp.int32, (rows, rows), 0)
    col = lax.broadcasted_iota(jnp.int32, (rows, rows), 1)
    across = jnp.broadcast_to(docs_ref[...].astype(F32), (rows, rows))
    down = jnp.sum(jnp.where(row == col, across, 0.0), axis=1, keepdims=True)
    allowed = jnp.where((across == down) & (col <= row), 1.0, 0.0)
    allowed = jnp.concatenate([allowed] * SIDE, axis=1)
    return jnp.concatenate([allowed] * (GROUP // SIDE), axis=0) > 0.5


def stacked(ref, k):
    wide = SIDE * HD
    groups = GROUP // SIDE
    return jnp.concatenate(
        [ref[:, (k * groups + g) * wide : (k * groups + g + 1) * wide] for g in range(groups)], axis=0
    )


def probs_kernel(places, factors, axis, *refs):
    cut_f, cut_b = refs[:2]
    pieces, refs = refs[2 : 2 + len(places)], refs[2 + len(places) :]
    old, _, hid_f, hid_b, docs_f, docs_b, total, weight, probs_f, probs_b, key_b = refs
    rows = hid_f.shape[0]
    total[...] = old[...]
    add_pieces(places, factors, axis, cut_f, cut_b, pieces, total, weight)
    keys = total[:, : KVH * HD].astype(BF16)
    ones = same_segment(rows)
    mask_f = allowed_mask(docs_f)
    mask_b = allowed_mask(docs_b)
    for k in range(KVH):
        key = beside(keys[rows:, k * HD : (k + 1) * HD])
        key_b[k] = key
        probs_b[k] = probabilities(stacked(hid_b, k), key, mask_b, ones, rows)
        key = beside(keys[:rows, k * HD : (k + 1) * HD])
        probs_f[k] = probabilities(stacked(hid_f, k), key, mask_f, ones, rows).astype(BF16)


def probs_call(cut_f, cut_b, group, factors, axis, state, hid_f, hid_b, docs):
    pieces, places = [p for p, _, _ in group], [(o, c) for _, o, c in group]
    rows = hid_f.shape[0]
    n = 2 + len(pieces)
    scores = (KVH, GROUP // SIDE * rows, SIDE * rows)
    return pl.pallas_call(
        functools.partial(probs_kernel, places, factors, axis),
        out_shape=(
            jax.ShapeDtypeStruct(state[0].shape, F32),
            jax.ShapeDtypeStruct(state[1].shape, BF16),
            jax.ShapeDtypeStruct(scores, BF16),
            jax.ShapeDtypeStruct(scores, F32),
            jax.ShapeDtypeStruct((KVH, SIDE * rows, SIDE * HD), BF16),
        ),
        input_output_aliases={n: 0, n + 1: 1},
        cost_estimate=pl.CostEstimate(flops=1 << 28, bytes_accessed=1 << 22, transcendentals=1 << 19),
        compiler_params=pltpu.CompilerParams(vmem_limit_bytes=24 << 20),
        name="probs",
    )(cut_f, cut_b, *pieces, *state, hid_f, hid_b, *docs)


def tail_kernel(places, factors, axis, *refs):
    cut_f, cut_b = refs[:2]
    pieces, refs = refs[2 : 2 + len(places)], refs[2 + len(places) :]
    (old, _, probs_f, probs_b, key_b, hid_b, u_ref, saved_ref, cot_ref, gain_ref, scale_ref), refs = (
        refs[:11], refs[11:])
    fwd_ref, back_ref, total, weight, grad_kv, grad_q = refs
    rows, width = u_ref.shape
    keys = KVH * HD
    groups = GROUP // SIDE
    wide = SIDE * HD

    total[...] = old[...]
    add_pieces(places, factors, axis, cut_f, cut_b, pieces, total, weight)
    values = total[:, keys:].astype(BF16)
    ones = same_segment(rows)
    for k in range(KVH):
        key = key_b[k]
        value = beside(values[rows:, k * HD : (k + 1) * HD])
        queries, grads = stacked(hid_b, k), stacked(cot_ref, k)
        probs = probs_b[k]
        grad_probs = dot(grads, value, ((1,), (1,))).astype(BF16).astype(F32)
        mean = segment_sum(probs * grad_probs, ones)
        grad_scores = (probs * (grad_probs - mean) * HD**-0.5).astype(BF16)
        grad_queries = dot(grad_scores, key).astype(BF16)
        for g in range(groups):
            at = (k * groups + g) * wide
            grad_q[:, at : at + wide] = grad_queries[g * rows : (g + 1) * rows]
        grad_key = diagonal(dot(grad_scores, queries, ((0,), (0,))), rows, HD)
        grad_value = diagonal(dot(probs.astype(BF16), grads, ((0,), (0,))), rows, HD)
        grad_kv[:, k * HD : (k + 1) * HD] = grad_key.astype(BF16)
        grad_kv[:, keys + k * HD : keys + (k + 1) * HD] = grad_value.astype(BF16)
    for k in range(KVH):
        value = beside(values[:rows, k * HD : (k + 1) * HD])
        mixed = dot(probs_f[k], value)
        for g in range(groups):
            at = (k * groups + g) * wide
            fwd_ref[:, at : at + wide] = (
                u_ref[:, at : at + wide].astype(F32) + mixed[g * rows : (g + 1) * rows]
            ).astype(BF16)
    grads = grad_kv[...]
    step = width // 9
    along = jnp.zeros((rows, 1), F32)
    for c in range(0, width, step):
        at = slice(c, c + step)
        through = dot(grads, weight[at, :], ((1,), (1,))) + grad_q[:, at].astype(F32)
        through = through.astype(BF16)
        grad_q[:, at] = through
        part = through.astype(F32) * gain_ref[:, at] * saved_ref[:, at].astype(F32)
        along = along + jnp.sum(part, axis=-1, keepdims=True)
    scale = scale_ref[:, :1]
    along = along * (scale * scale * scale) / width
    for c in range(0, width, step):
        at = slice(c, c + step)
        grad = grad_q[:, at].astype(F32) * gain_ref[:, at] * scale
        grad = (grad - saved_ref[:, at].astype(F32) * along).astype(BF16)
        back_ref[:, at] = (cot_ref[:, at].astype(F32) + grad.astype(F32)).astype(BF16)


def tail_call(cut_f, cut_b, group, factors, axis, state, probs_f, probs_b, key_b, hid_b,
              incoming, saved, cotangent, gain, scale_b):
    pieces, places = [p for p, _, _ in group], [(o, c) for _, o, c in group]
    rows, width = incoming.shape
    columns = state[0].shape[1]
    n = 2 + len(pieces)
    fwd_out, back_out, _, _ = pl.pallas_call(
        functools.partial(tail_kernel, places, factors, axis),
        out_shape=(
            jax.ShapeDtypeStruct((rows, width), BF16),
            jax.ShapeDtypeStruct((rows, width), BF16),
            jax.ShapeDtypeStruct(state[0].shape, F32),
            jax.ShapeDtypeStruct(state[1].shape, BF16),
        ),
        input_output_aliases={n: 2, n + 1: 3},
        scratch_shapes=[
            pltpu.VMEM((rows, columns), BF16),
            pltpu.VMEM((rows, width), BF16),
        ],
        cost_estimate=pl.CostEstimate(
            flops=2 * rows * width * columns, bytes_accessed=2 * width * columns, transcendentals=0
        ),
        compiler_params=pltpu.CompilerParams(vmem_limit_bytes=28 << 20),
        name="tail",
    )(cut_f, cut_b, *pieces, *state, probs_f, probs_b, key_b, hid_b, incoming, saved, cotangent,
      gain, scale_b)
    return fwd_out, back_out


def shifted(x, axis, factors, steps):
    n = lax.axis_size(axis)
    pairs = []
    for me in range(n):
        source, stride = 0, 1
        for size, step in zip(reversed(factors), reversed(steps)):
            source = source + (me // stride % size + step) % size * stride
            stride = stride * size
        pairs.append((source, me))
    return lax.ppermute(x, axis, pairs)


def grid_factors(mesh, axis):
    n = mesh.shape[axis]
    place = list(mesh.axis_names).index(axis)
    devices = mesh.devices
    line = devices[tuple(slice(None) if i == place else 0 for i in range(devices.ndim))]
    spots = [(*getattr(d, "coords", (i,)), getattr(d, "core_on_chip", 0)) for i, d in enumerate(line)]
    factors, stride = [], 1
    while stride < n:
        moved = [i for i in range(len(spots[0])) if spots[stride][i] != spots[0][i]][0]
        size = len({s[moved] for s in spots[::stride]})
        factors.insert(0, size)
        stride *= size
    return tuple(factors)


def on_device(factors, fwd_prev, saved, back_prev, fwd_docs, back_docs, gain, weight):
    sections = lax.axis_size("section")
    own = weight[0]
    ring = lambda x, by: lax.ppermute(x, "section", [(i, (i + by) % sections) for i in range(sections)])

    def move(x, *steps):
        return shifted(x, "fsdp", factors, steps)

    half = own.shape[1] // 2
    keys = lambda x: x[:, :half]
    values = lambda x: x[:, half:]
    if relayed(factors):
        y0 = move(own, 0, 1, 0)
        z1 = move(own, 1, 0, 0)
        own_k, own_v = keys(own), values(own)
        z3k = move(own_k, 3, 0, 0)
        incoming = ring(fwd_prev[0], 1)
        cotangent = ring(back_prev[0], -1)
        c0 = move(own, 0, 0, 1)
        y1 = move(z1, 0, 1, 0)
        z2k = move(keys(z1), 1, 0, 0)
        z2v = move(values(z1), 1, 0, 0)
        z3v = move(own_v, 3, 0, 0)
        z3yv = move(values(y0), 3, 0, 0)
        y3k = move(z3k, 0, 1, 0)
        y2k = move(z2k, 0, 1, 0)
        y2v = move(z2v, 0, 1, 0)

        def both(x, z, y, column):
            return [(x, (z, y, 0), column), (move(x, 0, 0, 1), (z, y, 1), column)]

        groups = [
            [(own, (0, 0, 0), 0), (c0, (0, 0, 1), 0), *both(y0, 0, 1, 0), *both(z1, 1, 0, 0)],
            [*both(z3k, 3, 0, 0), *both(y1, 1, 1, 0), *both(z2k, 2, 0, 0)],
            [*both(z2v, 2, 0, half), *both(y3k, 3, 1, 0)],
            both(y2k, 2, 1, 0),
            [*both(z3v, 3, 0, half), *both(z3yv, 3, 1, half), *both(y2v, 2, 1, half)],
        ]
        shape, axis = factors, "fsdp"
    else:
        incoming = ring(fwd_prev[0], 1)
        cotangent = ring(back_prev[0], -1)
        full = lax.all_gather(own, "fsdp", axis=0, tiled=True)
        top, low = jnp.split(full, 2)
        groups = [[(top, (0,), 0)], [(keys(low), (1,), 0)], [(values(low), (1,), half)]]
        shape, axis = (2,), None
    pieces = 1
    for size in shape:
        pieces *= size
    hid_b, cut_b, scale_b = norm_call(saved[0], gain, pieces)
    hid_f, cut_f, _ = norm_call(incoming, gain, pieces)
    state = None
    for group in groups[:-2]:
        state = keyval_call(cut_f, cut_b, group, shape, axis, state, (saved.shape[2], own.shape[1]))
    *state, probs_f, probs_b, key_b = probs_call(
        cut_f, cut_b, groups[-2], shape, axis, state, hid_f, hid_b, (fwd_docs, back_docs)
    )
    fwd_out, back_out = tail_call(
        cut_f, cut_b, groups[-1], shape, axis, state, probs_f, probs_b, key_b, hid_b,
        incoming, saved[0], cotangent, gain, scale_b,
    )
    return (fwd_out[None], back_out[None])


def relayed(factors):
    return len(factors) == 3 and factors[0] == 4 and factors[1:] == (2, 2)


def solution(mesh):
    in_specs = (
        P("section", "fsdp", None),
        P("section", "fsdp", None),
        P("section", "fsdp", None),
        P("section", "fsdp"),
        P("section", "fsdp"),
        P("section", None),
        P("section", "fsdp", None),
    )
    out_specs = (P("section", "fsdp", None), P("section", "fsdp", None))
    factors = grid_factors(mesh, "fsdp")
    return jax.shard_map(
        functools.partial(on_device, factors),
        mesh=mesh, in_specs=in_specs, out_specs=out_specs, check_vma=False,
    )
```

```python
import functools

import jax
import jax.numpy as jnp
from jax import lax
from jax.experimental import pallas as pl
from jax.experimental.pallas import tpu as pltpu
from jax.sharding import PartitionSpec as P


HD = 96
KVH = 4
GROUP = 12
SIDE = 4
EPSILON = 1e-05

F32 = jnp.float32
BF16 = jnp.bfloat16


def dot(a, b, over=((1,), (0,))):
    return lax.dot_general(a, b, (over, ((), ())), preferred_element_type=F32)


def norm_kernel(u_ref, gain_ref, hidden_ref, cut_ref, *extra):
    rows, width = u_ref.shape
    parts, _, depth = cut_ref.shape
    step = width // 9
    total = jnp.zeros((rows, 1), F32)
    for c in range(0, width, step):
        values = u_ref[:, c : c + step].astype(F32)
        total = total + jnp.sum(values * values, axis=-1, keepdims=True)
    scale = lax.rsqrt(total / width + EPSILON)
    for c in range(0, width, step):
        at = slice(c, c + step)
        values = u_ref[:, at].astype(F32)
        hidden_ref[:, at] = (values * scale * gain_ref[:, at]).astype(BF16)
    for p in range(parts):
        cut_ref[p] = hidden_ref[:, p * depth : (p + 1) * depth]
    if extra:
        scale_ref, gain_scale, gain_values, turned = extra
        scale_ref[...] = jnp.broadcast_to(scale, scale_ref.shape)
        for c in range(0, width, step):
            at = slice(c, c + step)
            gain_scale[:, at] = gain_ref[:, at] * scale
            gain_values[:, at] = gain_ref[:, at] * u_ref[:, at].astype(F32)
        for k in range(KVH):
            turned[k] = stacked(hidden_ref, k).T


def norm_call(rows_in, gain, parts, backward):
    rows, width = rows_in.shape
    out = [
        jax.ShapeDtypeStruct((rows, width), BF16),
        jax.ShapeDtypeStruct((parts, rows, width // parts), BF16),
    ]
    if backward:
        out += [
            jax.ShapeDtypeStruct((rows, 128), F32),
            jax.ShapeDtypeStruct((rows, width), F32),
            jax.ShapeDtypeStruct((rows, width), F32),
            jax.ShapeDtypeStruct((KVH, SIDE * HD, GROUP // SIDE * rows), BF16),
        ]
    return pl.pallas_call(
        norm_kernel,
        out_shape=out,
        cost_estimate=pl.CostEstimate(
            flops=6 * rows * width, bytes_accessed=6 * rows * width, transcendentals=rows
        ),
        compiler_params=pltpu.CompilerParams(vmem_limit_bytes=10 << 20),
        name="norm",
    )(rows_in, gain)


def grid_place(offset, factors, axis):
    me = 0 if axis is None else lax.axis_index(axis)
    index, stride = 0, 1
    beyond = 1
    for size in factors[len(offset) :]:
        beyond = beyond * size
    for size, away in zip(reversed(factors[: len(offset)]), reversed(offset)):
        mine = lax.rem(lax.div(me, beyond * stride), size)
        index = index + lax.rem(mine + away, size) * stride
        stride = stride * size
    return index


def add_pieces(items, factors, axis, cut_f, cut_b, pieces, total, weight):
    pieces = list(pieces)
    for offset, column, count in items:
        at = grid_place(offset, factors, axis)
        mine = lax.rem(lax.axis_index(axis), count) if count > 1 else 0
        depth, width = pieces[0].shape
        columns = slice(column, column + width)
        start = pl.multiple_of(at * (count * depth), 16)
        for i in range(count):
            row = start + lax.rem(mine + i, count) * depth
            weight[pl.ds(pl.multiple_of(row, 16), depth), columns] = pieces.pop(0)[...]
        value = weight[pl.ds(start, count * depth), columns]
        total[:, columns] += dot(jnp.concatenate([cut_f[at], cut_b[at]], axis=0), value)


def flat(group):
    return [p for item in group for p in item[0]], [(o, c, len(p)) for p, o, c in group]


def keyval_kernel(items, count, factors, axis, first, *refs):
    cut_f, cut_b = refs[:2]
    pieces, (total, weight) = refs[2 : 2 + count], refs[-2:]
    total[...] = jnp.zeros_like(total) if first else refs[2 + count][...]
    add_pieces(items, factors, axis, cut_f, cut_b, pieces, total, weight)


def keyval_call(cut_f, cut_b, group, factors, axis, state, shape):
    pieces, items = flat(group)
    rows = 2 * cut_f.shape[1]
    work = rows * sum(p.size for p in pieces)
    n = 2 + len(pieces)
    return pl.pallas_call(
        functools.partial(keyval_kernel, items, len(pieces), factors, axis, state is None),
        out_shape=(
            jax.ShapeDtypeStruct((rows, shape[1]), F32),
            jax.ShapeDtypeStruct(shape, BF16),
        ),
        input_output_aliases={} if state is None else {n: 0, n + 1: 1},
        cost_estimate=pl.CostEstimate(
            flops=2 * work, bytes_accessed=work // rows * 2, transcendentals=0
        ),
        compiler_params=pltpu.CompilerParams(vmem_limit_bytes=20 << 20),
        name="keyval",
    )(cut_f, cut_b, *pieces, *(() if state is None else state))


def beside(x):
    _, width = x.shape
    wide = jnp.concatenate([x] * SIDE, axis=1)
    lane = lax.broadcasted_iota(jnp.int32, wide.shape, 1)
    blocks = [
        jnp.where((lane >= j * width) & (lane < (j + 1) * width), wide, jnp.zeros_like(wide))
        for j in range(SIDE)
    ]
    return jnp.concatenate(blocks, axis=0)


def diagonal(x, rows, width):
    total = x[:rows, :width]
    for j in range(1, SIDE):
        total = total + x[j * rows : (j + 1) * rows, j * width : (j + 1) * width]
    return total


def same_segment(rows):
    size = SIDE * rows
    a = lax.broadcasted_iota(jnp.int32, (size, size), 0) // rows
    b = lax.broadcasted_iota(jnp.int32, (size, size), 1) // rows
    return (a == b).astype(F32).astype(BF16)


def segment_sum(x, ones):
    high = x.astype(BF16)
    low = (x - high.astype(F32)).astype(BF16)
    return dot(high, ones) + dot(low, ones)


def segment_max(x, rows):
    lane = lax.broadcasted_iota(jnp.int32, x.shape, 1)
    result = None
    for j in range(SIDE):
        inside = (lane >= j * rows) & (lane < (j + 1) * rows)
        top = jnp.max(jnp.where(inside, x, -3e38), axis=-1, keepdims=True)
        result = top + jnp.zeros_like(x) if result is None else jnp.where(lane >= j * rows, top, result)
    return result


def probabilities(queries, keys, allowed, ones, rows):
    scores = dot(queries, keys, ((1,), (1,))) * HD**-0.5
    scores = jnp.where(allowed, scores, -1e30)
    powers = jnp.exp(scores - segment_max(scores, rows))
    return powers / segment_sum(powers, ones)


def allowed_mask(docs_ref):
    rows = docs_ref.shape[1]
    row = lax.broadcasted_iota(jnp.int32, (rows, rows), 0)
    col = lax.broadcasted_iota(jnp.int32, (rows, rows), 1)
    across = jnp.broadcast_to(docs_ref[...].astype(F32), (rows, rows))
    down = jnp.sum(jnp.where(row == col, across, 0.0), axis=1, keepdims=True)
    allowed = jnp.where((across == down) & (col <= row), 1.0, 0.0)
    allowed = jnp.concatenate([allowed] * SIDE, axis=1)
    return jnp.concatenate([allowed] * (GROUP // SIDE), axis=0) > 0.5


def stacked(ref, k):
    wide = SIDE * HD
    groups = GROUP // SIDE
    return jnp.concatenate(
        [ref[:, (k * groups + g) * wide : (k * groups + g + 1) * wide] for g in range(groups)], axis=0
    )


def probs_kernel(items, count, factors, axis, *refs):
    cut_f, cut_b = refs[:2]
    pieces, refs = refs[2 : 2 + count], refs[2 + count :]
    old, _, hid_f, hid_b, docs_f, docs_b, total, weight, probs_f, probs_b, key_b = refs
    rows = hid_f.shape[0]
    total[...] = old[...]
    add_pieces(items, factors, axis, cut_f, cut_b, pieces, total, weight)
    keys = total[:, : KVH * HD].astype(BF16)
    ones = same_segment(rows)
    mask_f = allowed_mask(docs_f)
    mask_b = allowed_mask(docs_b)
    for k in range(KVH):
        key = beside(keys[rows:, k * HD : (k + 1) * HD])
        key_b[k] = key
        probs_b[k] = probabilities(stacked(hid_b, k), key, mask_b, ones, rows)
        key = beside(keys[:rows, k * HD : (k + 1) * HD])
        probs_f[k] = probabilities(stacked(hid_f, k), key, mask_f, ones, rows).astype(BF16)


def probs_call(cut_f, cut_b, group, factors, axis, state, hid_f, hid_b, docs):
    pieces, items = flat(group)
    rows = hid_f.shape[0]
    n = 2 + len(pieces)
    scores = (KVH, GROUP // SIDE * rows, SIDE * rows)
    return pl.pallas_call(
        functools.partial(probs_kernel, items, len(pieces), factors, axis),
        out_shape=(
            jax.ShapeDtypeStruct(state[0].shape, F32),
            jax.ShapeDtypeStruct(state[1].shape, BF16),
            jax.ShapeDtypeStruct(scores, BF16),
            jax.ShapeDtypeStruct(scores, F32),
            jax.ShapeDtypeStruct((KVH, SIDE * rows, SIDE * HD), BF16),
        ),
        input_output_aliases={n: 0, n + 1: 1},
        cost_estimate=pl.CostEstimate(flops=1 << 28, bytes_accessed=1 << 22, transcendentals=1 << 19),
        compiler_params=pltpu.CompilerParams(vmem_limit_bytes=24 << 20),
        name="probs",
    )(cut_f, cut_b, *pieces, *state, hid_f, hid_b, *docs)


def mid_kernel(items, count, factors, axis, *refs):
    cut_f, cut_b = refs[:2]
    pieces, refs = refs[2 : 2 + count], refs[2 + count :]
    old, _, probs_b, cot_ref, total, weight, grad_v, through, turned = refs
    rows = cot_ref.shape[0]
    keys = KVH * HD
    depth = weight.shape[0]
    step = depth // 9
    total[...] = old[...]
    add_pieces(items, factors, axis, cut_f, cut_b, pieces, total, weight)
    for k in range(KVH):
        grad = dot(probs_b[k].astype(BF16), stacked(cot_ref, k), ((0,), (0,)))
        grad_v[:, k * HD : (k + 1) * HD] = diagonal(grad, rows, HD).astype(BF16)
    grads = grad_v[...]
    for c in range(0, depth, step):
        at = slice(c, c + step)
        through[:, at] = dot(grads, weight[at, keys:], ((1,), (1,)))
        turned[:, at] = weight[at, :keys].T


def mid_call(cut_f, cut_b, group, factors, axis, state, probs_b, cotangent):
    pieces, items = flat(group)
    rows, width = cotangent.shape
    n = 2 + len(pieces)
    return pl.pallas_call(
        functools.partial(mid_kernel, items, len(pieces), factors, axis),
        out_shape=(
            jax.ShapeDtypeStruct(state[0].shape, F32),
            jax.ShapeDtypeStruct(state[1].shape, BF16),
            jax.ShapeDtypeStruct((rows, KVH * HD), BF16),
            jax.ShapeDtypeStruct((rows, width), F32),
            jax.ShapeDtypeStruct((KVH * HD, width), BF16),
        ),
        input_output_aliases={n: 0, n + 1: 1},
        cost_estimate=pl.CostEstimate(flops=1 << 28, bytes_accessed=1 << 22, transcendentals=0),
        compiler_params=pltpu.CompilerParams(vmem_limit_bytes=28 << 20),
        name="mid",
    )(cut_f, cut_b, *pieces, *state, probs_b, cotangent)


def place_columns(ref, at, depth, value):
    if depth % 128 == 0:
        ref[:, pl.ds(pl.multiple_of(at * depth, 128), depth)] = value
        return
    low = depth * 2 // 128 * 128 // 2 // 128 * 128
    base = lax.div(at, 2) * (2 * depth)

    @pl.when(lax.rem(at, 2) == 0)
    def _():
        ref.at[:, pl.ds(pl.multiple_of(base, 128), 2 * depth)][:, :depth] = value

    @pl.when(lax.rem(at, 2) == 1)
    def _():
        ref.at[:, pl.ds(pl.multiple_of(base + low, 128), 2 * depth - low)][:, depth - low :] = value


def tail_kernel(items, count, factors, axis, *refs):
    cut_f, cut_b = refs[:2]
    pieces, refs = refs[2 : 2 + count], refs[2 + count :]
    (total_ref, _, half_ref, probs_f, probs_b, key_b, grad_v, turned, queries, u_ref, saved_ref,
     cot_ref, scale_ref, gain_scale, gain_values), refs = refs[:15], refs[15:]
    fwd_ref, back_ref, weight, through, total, grad_q, grad_k = refs
    rows, width = u_ref.shape
    keys = KVH * HD
    groups = GROUP // SIDE
    wide = SIDE * HD

    total[...] = total_ref[...]
    add_pieces(items, factors, axis, cut_f, cut_b, pieces, total, weight)
    values = total[:, keys:].astype(BF16)
    ones = same_segment(rows)
    for k in range(KVH):
        value = beside(values[rows:, k * HD : (k + 1) * HD])
        probs = probs_b[k]
        grad_probs = dot(stacked(cot_ref, k), value, ((1,), (1,))).astype(BF16).astype(F32)
        mean = segment_sum(probs * grad_probs, ones)
        grad_scores = (probs * (grad_probs - mean) * HD**-0.5).astype(BF16)
        grad_queries = dot(grad_scores, key_b[k]).astype(BF16)
        for g in range(groups):
            at = (k * groups + g) * wide
            grad_q[:, at : at + wide] = grad_queries[g * rows : (g + 1) * rows]
        grad = dot(queries[k], grad_scores)
        part = grad[:HD, :rows]
        for j in range(1, SIDE):
            part = part + grad[j * HD : (j + 1) * HD, j * rows : (j + 1) * rows]
        grad_k[k * HD : (k + 1) * HD, :] = part
    for k in range(KVH):
        mixed = dot(probs_f[k], beside(values[:rows, k * HD : (k + 1) * HD]))
        for g in range(groups):
            at = (k * groups + g) * wide
            fwd_ref[:, at : at + wide] = (
                u_ref[:, at : at + wide].astype(F32) + mixed[g * rows : (g + 1) * rows]
            ).astype(BF16)
    for offset, column, pair in items:
        at = grid_place(offset, factors, axis)
        depth = pair * pieces[0].shape[0]
        value = weight[pl.ds(pl.multiple_of(at * depth, 16), depth), column:]
        place_columns(through, at, depth, dot(grad_v[...], value, ((1,), (1,))))
    grads = grad_k[...].T.astype(BF16)
    step = width // 9
    along = jnp.zeros((rows, 1), F32)
    for c in range(0, width, step):
        at = slice(c, c + step)
        full = dot(grads, turned[:, at]) + through[:, at] + grad_q[:, at].astype(F32)
        full = full.astype(BF16)
        grad_q[:, at] = full
        along = along + jnp.sum(full.astype(F32) * gain_values[:, at], axis=-1, keepdims=True)
    scale = scale_ref[:, :1]
    along = along * (scale * scale * scale) / width
    for c in range(0, width, step):
        at = slice(c, c + step)
        grad = grad_q[:, at].astype(F32) * gain_scale[:, at] - saved_ref[:, at].astype(F32) * along
        back_ref[:, at] = cot_ref[:, at] + grad.astype(BF16)


def tail_call(cut_f, cut_b, group, factors, axis, state, through, *others):
    pieces, items = flat(group)
    rows, width = through.shape
    n = 2 + len(pieces)
    fwd_out, back_out, _, _ = pl.pallas_call(
        functools.partial(tail_kernel, items, len(pieces), factors, axis),
        out_shape=(
            jax.ShapeDtypeStruct((rows, width), BF16),
            jax.ShapeDtypeStruct((rows, width), BF16),
            jax.ShapeDtypeStruct(state[1].shape, BF16),
            jax.ShapeDtypeStruct(through.shape, F32),
        ),
        input_output_aliases={n + 1: 2, n + 2: 3},
        scratch_shapes=[
            pltpu.VMEM(state[0].shape, F32),
            pltpu.VMEM((rows, width), BF16),
            pltpu.VMEM((KVH * HD, rows), F32),
        ],
        cost_estimate=pl.CostEstimate(flops=1 << 29, bytes_accessed=1 << 23, transcendentals=0),
        compiler_params=pltpu.CompilerParams(vmem_limit_bytes=30 << 20),
        name="tail",
    )(cut_f, cut_b, *pieces, *state, through, *others)
    return fwd_out, back_out


def shifted(x, axis, factors, steps):
    n = lax.axis_size(axis)
    pairs = []
    for me in range(n):
        source, stride = 0, 1
        for size, step in zip(reversed(factors), reversed(steps)):
            source = source + (me // stride % size + step) % size * stride
            stride = stride * size
        pairs.append((source, me))
    return lax.ppermute(x, axis, pairs)


def grid_factors(mesh, axis):
    n = mesh.shape[axis]
    place = list(mesh.axis_names).index(axis)
    devices = mesh.devices
    line = devices[tuple(slice(None) if i == place else 0 for i in range(devices.ndim))]
    spots = [(*getattr(d, "coords", (i,)), getattr(d, "core_on_chip", 0)) for i, d in enumerate(line)]
    factors, stride = [], 1
    while stride < n:
        moved = [i for i in range(len(spots[0])) if spots[stride][i] != spots[0][i]][0]
        size = len({s[moved] for s in spots[::stride]})
        factors.insert(0, size)
        stride *= size
    return tuple(factors)


def on_device(factors, fwd_prev, saved, back_prev, fwd_docs, back_docs, gain, weight):
    sections = lax.axis_size("section")
    own = weight[0]
    ring = lambda x, by: lax.ppermute(x, "section", [(i, (i + by) % sections) for i in range(sections)])

    def move(x, *steps):
        return shifted(x, "fsdp", factors, steps)

    half = own.shape[1] // 2
    keys = lambda x: x[:, :half]
    values = lambda x: x[:, half:]
    if relayed(factors):
        z1 = move(own, 1, 0, 0)
        y0 = move(own, 0, 1, 0)
        own_k, own_v = keys(own), values(own)
        z3k = move(own_k, 3, 0, 0)
        incoming = ring(fwd_prev[0], 1)
        cotangent = ring(back_prev[0], -1)
        c0 = move(own, 0, 0, 1)
        z1k, z1v = keys(z1), values(z1)
        y1k = move(z1k, 0, 1, 0)
        y1v = move(z1v, 0, 1, 0)
        z2k = move(z1k, 1, 0, 0)
        z2v = move(z1v, 1, 0, 0)
        z3v = move(own_v, 3, 0, 0)
        z3yv = move(values(y0), 3, 0, 0)
        y3k = move(z3k, 0, 1, 0)
        y2k = move(z2k, 0, 1, 0)
        y2v = move(z2v, 0, 1, 0)

        def both(x, z, y, column=0):
            return ([x, move(x, 0, 0, 1)], (z, y), column)

        groups = [
            ("keyval", [([own, c0], (0, 0), 0), both(y0, 0, 1), both(z1, 1, 0)]),
            ("keyval", [both(z3k, 3, 0), both(y1k, 1, 1), both(z2k, 2, 0),
                        both(y3k, 3, 1)]),
            ("probs", [both(y2k, 2, 1)]),
            ("mid", [both(z2v, 2, 0, half), both(y1v, 1, 1, half),
                     both(z3v, 3, 0, half)]),
            ("tail", [both(z3yv, 3, 1, half), both(y2v, 2, 1, half)]),
        ]
        parts, grid, axis = factors[0] * factors[1], factors, "fsdp"
    else:
        incoming = ring(fwd_prev[0], 1)
        cotangent = ring(back_prev[0], -1)
        full = lax.all_gather(own, "fsdp", axis=0, tiled=True)
        first, second, third, fourth = jnp.split(full, 4)
        groups = [
            ("keyval", [([first], (0,), 0), ([second], (1,), 0), ([keys(third)], (2,), 0)]),
            ("probs", [([keys(fourth)], (3,), 0)]),
            ("mid", [([values(third)], (2,), half)]),
            ("tail", [([values(fourth)], (3,), half)]),
        ]
        parts, grid, axis = 4, (4,), None
    hid_b, cut_b, scale_b, gain_scale, gain_values, turned_b = norm_call(saved[0], gain, parts, True)
    hid_f, cut_f = norm_call(incoming, gain, parts, False)
    state = None
    for kind, group in groups[:-1]:
        if kind == "probs":
            *state, probs_f, probs_b, key_b = probs_call(
                cut_f, cut_b, group, grid, axis, state, hid_f, hid_b, (fwd_docs, back_docs)
            )
        elif kind == "mid":
            *state, grad_v, through, turned = mid_call(
                cut_f, cut_b, group, grid, axis, state, probs_b, cotangent
            )
        else:
            state = keyval_call(
                cut_f, cut_b, group, grid, axis, state, (saved.shape[2], own.shape[1])
            )
    fwd_out, back_out = tail_call(
        cut_f, cut_b, groups[-1][1], grid, axis, state, through, probs_f, probs_b, key_b, grad_v,
        turned, turned_b, incoming, saved[0], cotangent, scale_b, gain_scale, gain_values,
    )
    return (fwd_out[None], back_out[None])


def relayed(factors):
    return len(factors) == 3 and factors[0] == 4 and factors[1:] == (2, 2)


def solution(mesh):
    in_specs = (
        P("section", "fsdp", None),
        P("section", "fsdp", None),
        P("section", "fsdp", None),
        P("section", "fsdp"),
        P("section", "fsdp"),
        P("section", None),
        P("section", "fsdp", None),
    )
    out_specs = (P("section", "fsdp", None), P("section", "fsdp", None))
    factors = grid_factors(mesh, "fsdp")
    return jax.shard_map(
        functools.partial(on_device, factors),
        mesh=mesh, in_specs=in_specs, out_specs=out_specs, check_vma=False,
    )
```

```python
import functools

import jax
import jax.numpy as jnp
from jax import lax
from jax.experimental import pallas as pl
from jax.experimental.pallas import tpu as pltpu
from jax.sharding import PartitionSpec as P


HD = 96
KVH = 4
GROUP = 12
SIDE = 4
EPSILON = 1e-05

F32 = jnp.float32
BF16 = jnp.bfloat16


def dot(a, b, over=((1,), (0,))):
    return lax.dot_general(a, b, (over, ((), ())), preferred_element_type=F32)


def norm_kernel(u_ref, gain_ref, hidden_ref, cut_ref, *extra):
    rows, width = u_ref.shape
    parts, _, depth = cut_ref.shape
    step = width // 9
    total = jnp.zeros((rows, 1), F32)
    for c in range(0, width, step):
        values = u_ref[:, c : c + step].astype(F32)
        total = total + jnp.sum(values * values, axis=-1, keepdims=True)
    scale = lax.rsqrt(total / width + EPSILON)
    for c in range(0, width, step):
        at = slice(c, c + step)
        values = u_ref[:, at].astype(F32)
        hidden_ref[:, at] = (values * scale * gain_ref[:, at]).astype(BF16)
    for p in range(parts):
        cut_ref[p] = hidden_ref[:, p * depth : (p + 1) * depth]
    if extra:
        scale_ref, gain_scale, gain_values, turned = extra
        scale_ref[...] = jnp.broadcast_to(scale, scale_ref.shape)
        for c in range(0, width, step):
            at = slice(c, c + step)
            gain_scale[:, at] = gain_ref[:, at] * scale
            gain_values[:, at] = gain_ref[:, at] * u_ref[:, at].astype(F32)
        for k in range(KVH):
            turned[k] = stacked(hidden_ref, k).T


def norm_call(rows_in, gain, parts, backward):
    rows, width = rows_in.shape
    out = [
        jax.ShapeDtypeStruct((rows, width), BF16),
        jax.ShapeDtypeStruct((parts, rows, width // parts), BF16),
    ]
    if backward:
        out += [
            jax.ShapeDtypeStruct((rows, 128), F32),
            jax.ShapeDtypeStruct((rows, width), F32),
            jax.ShapeDtypeStruct((rows, width), F32),
            jax.ShapeDtypeStruct((KVH, SIDE * HD, GROUP // SIDE * rows), BF16),
        ]
    return pl.pallas_call(
        norm_kernel,
        out_shape=out,
        cost_estimate=pl.CostEstimate(
            flops=6 * rows * width, bytes_accessed=6 * rows * width, transcendentals=rows
        ),
        compiler_params=pltpu.CompilerParams(vmem_limit_bytes=10 << 20),
        name="norm",
    )(rows_in, gain)


def grid_place(offset, factors, axis):
    me = 0 if axis is None else lax.axis_index(axis)
    index, stride = 0, 1
    beyond = 1
    for size in factors[len(offset) :]:
        beyond = beyond * size
    for size, away in zip(reversed(factors[: len(offset)]), reversed(offset)):
        mine = lax.rem(lax.div(me, beyond * stride), size)
        index = index + lax.rem(mine + away, size) * stride
        stride = stride * size
    return index


def add_pieces(items, factors, axis, cut_f, cut_b, pieces, total, weight):
    pieces = list(pieces)
    for offset, column, count in items:
        at = grid_place(offset, factors, axis)
        mine = lax.rem(lax.axis_index(axis), count) if count > 1 else 0
        depth, width = pieces[0].shape
        columns = slice(column, column + width)
        start = pl.multiple_of(at * (count * depth), 16)
        for i in range(count):
            row = start + lax.rem(mine + i, count) * depth
            weight[pl.ds(pl.multiple_of(row, 16), depth), columns] = pieces.pop(0)[...]
        value = weight[pl.ds(start, count * depth), columns]
        total[:, columns] += dot(jnp.concatenate([cut_f[at], cut_b[at]], axis=0), value)


def flat(group):
    return [p for item in group for p in item[0]], [(o, c, len(p)) for p, o, c in group]


def keyval_kernel(items, count, factors, axis, first, *refs):
    cut_f, cut_b = refs[:2]
    pieces, (total, weight) = refs[2 : 2 + count], refs[-2:]
    total[...] = jnp.zeros_like(total) if first else refs[2 + count][...]
    add_pieces(items, factors, axis, cut_f, cut_b, pieces, total, weight)


def keyval_call(cut_f, cut_b, group, factors, axis, state, shape):
    pieces, items = flat(group)
    rows = 2 * cut_f.shape[1]
    work = rows * sum(p.size for p in pieces)
    n = 2 + len(pieces)
    return pl.pallas_call(
        functools.partial(keyval_kernel, items, len(pieces), factors, axis, state is None),
        out_shape=(
            jax.ShapeDtypeStruct((rows, shape[1]), F32),
            jax.ShapeDtypeStruct(shape, BF16),
        ),
        input_output_aliases={} if state is None else {n: 0, n + 1: 1},
        cost_estimate=pl.CostEstimate(
            flops=2 * work, bytes_accessed=work // rows * 2, transcendentals=0
        ),
        compiler_params=pltpu.CompilerParams(vmem_limit_bytes=20 << 20),
        name="keyval",
    )(cut_f, cut_b, *pieces, *(() if state is None else state))


def beside(x):
    _, width = x.shape
    wide = jnp.concatenate([x] * SIDE, axis=1)
    lane = lax.broadcasted_iota(jnp.int32, wide.shape, 1)
    blocks = [
        jnp.where((lane >= j * width) & (lane < (j + 1) * width), wide, jnp.zeros_like(wide))
        for j in range(SIDE)
    ]
    return jnp.concatenate(blocks, axis=0)


def diagonal(x, rows, width):
    total = x[:rows, :width]
    for j in range(1, SIDE):
        total = total + x[j * rows : (j + 1) * rows, j * width : (j + 1) * width]
    return total


def same_segment(rows):
    size = SIDE * rows
    a = lax.broadcasted_iota(jnp.int32, (size, size), 0) // rows
    b = lax.broadcasted_iota(jnp.int32, (size, size), 1) // rows
    return (a == b).astype(F32).astype(BF16)


def segment_sum(x, ones):
    high = x.astype(BF16)
    low = (x - high.astype(F32)).astype(BF16)
    return dot(high, ones) + dot(low, ones)


def segment_max(x, rows):
    tiles = []
    for start in range(0, x.shape[1], 128):
        tile = x[:, start : start + 128]
        lane = lax.broadcasted_iota(jnp.int32, tile.shape, 1)
        top = None
        for low in range(0, 128, rows):
            inside = (lane >= low) & (lane < low + rows)
            part = jnp.max(jnp.where(inside, tile, -3e38), axis=-1, keepdims=True)
            top = jnp.broadcast_to(part, tile.shape) if top is None else jnp.where(lane >= low, part, top)
        tiles.append(top)
    return jnp.concatenate(tiles, axis=1)


def staggered(stages, count):
    for step in range(count + len(stages) - 1):
        for i, stage in enumerate(stages):
            if 0 <= step - i < count:
                stage(step - i)


def allowed_mask(docs_ref):
    rows = docs_ref.shape[1]
    row = lax.broadcasted_iota(jnp.int32, (rows, rows), 0)
    col = lax.broadcasted_iota(jnp.int32, (rows, rows), 1)
    across = jnp.broadcast_to(docs_ref[...].astype(F32), (rows, rows))
    down = jnp.sum(jnp.where(row == col, across, 0.0), axis=1, keepdims=True)
    allowed = jnp.where((across == down) & (col <= row), 1.0, 0.0)
    allowed = jnp.concatenate([allowed] * SIDE, axis=1)
    return jnp.concatenate([allowed] * (GROUP // SIDE), axis=0) > 0.5


def stacked(ref, k):
    wide = SIDE * HD
    groups = GROUP // SIDE
    return jnp.concatenate(
        [ref[:, (k * groups + g) * wide : (k * groups + g + 1) * wide] for g in range(groups)], axis=0
    )


def probs_kernel(items, count, factors, axis, *refs):
    cut_f, cut_b = refs[:2]
    pieces, refs = refs[2 : 2 + count], refs[2 + count :]
    old, _, hid_f, hid_b, docs_f, docs_b, total, weight, probs_f, probs_b, key_b = refs
    rows = hid_f.shape[0]
    total[...] = old[...]
    add_pieces(items, factors, axis, cut_f, cut_b, pieces, total, weight)
    keys = total[:, : KVH * HD].astype(BF16)
    across = keys.T
    ones = same_segment(rows)
    masks = (allowed_mask(docs_f), allowed_mask(docs_b))
    held = {}

    def score(n):
        k, back = n // 2, 1 - n % 2
        key = beside(across[k * HD : (k + 1) * HD, back * rows : (back + 1) * rows])
        held[n] = dot(stacked((hid_f, hid_b)[back], k), key) * HD**-0.5
        if back:
            key_b[k] = beside(keys[rows:, k * HD : (k + 1) * HD])

    def power(n):
        scores = jnp.where(masks[1 - n % 2], held[n], -1e30)
        held[n] = jnp.exp(scores - segment_max(scores, rows))

    def divide(n):
        powers = held.pop(n)
        probs = powers * (1.0 / segment_sum(powers, ones))
        if n % 2 == 0:
            probs_b[n // 2] = probs
        else:
            probs_f[n // 2] = probs.astype(BF16)

    staggered((score, power, divide), 2 * KVH)


def probs_call(cut_f, cut_b, group, factors, axis, state, hid_f, hid_b, docs):
    pieces, items = flat(group)
    rows = hid_f.shape[0]
    n = 2 + len(pieces)
    scores = (KVH, GROUP // SIDE * rows, SIDE * rows)
    return pl.pallas_call(
        functools.partial(probs_kernel, items, len(pieces), factors, axis),
        out_shape=(
            jax.ShapeDtypeStruct(state[0].shape, F32),
            jax.ShapeDtypeStruct(state[1].shape, BF16),
            jax.ShapeDtypeStruct(scores, BF16),
            jax.ShapeDtypeStruct(scores, F32),
            jax.ShapeDtypeStruct((KVH, SIDE * rows, SIDE * HD), BF16),
        ),
        input_output_aliases={n: 0, n + 1: 1},
        cost_estimate=pl.CostEstimate(flops=1 << 28, bytes_accessed=1 << 22, transcendentals=1 << 19),
        compiler_params=pltpu.CompilerParams(vmem_limit_bytes=24 << 20),
        name="probs",
    )(cut_f, cut_b, *pieces, *state, hid_f, hid_b, *docs)


def mid_kernel(items, count, factors, axis, *refs):
    cut_f, cut_b = refs[:2]
    pieces, refs = refs[2 : 2 + count], refs[2 + count :]
    old, _, probs_b, cot_ref, total, weight, grad_v, through, turned = refs
    rows = cot_ref.shape[0]
    keys = KVH * HD
    depth = weight.shape[0]
    step = depth // 9
    total[...] = old[...]
    add_pieces(items, factors, axis, cut_f, cut_b, pieces, total, weight)
    for k in range(KVH):
        grad = dot(probs_b[k].astype(BF16), stacked(cot_ref, k), ((0,), (0,)))
        grad_v[:, k * HD : (k + 1) * HD] = diagonal(grad, rows, HD).astype(BF16)
    grads = grad_v[...]
    for c in range(0, depth, step):
        at = slice(c, c + step)
        through[:, at] = dot(grads, weight[at, keys:], ((1,), (1,)))
        turned[:, at] = weight[at, :keys].T


def mid_call(cut_f, cut_b, group, factors, axis, state, probs_b, cotangent):
    pieces, items = flat(group)
    rows, width = cotangent.shape
    n = 2 + len(pieces)
    return pl.pallas_call(
        functools.partial(mid_kernel, items, len(pieces), factors, axis),
        out_shape=(
            jax.ShapeDtypeStruct(state[0].shape, F32),
            jax.ShapeDtypeStruct(state[1].shape, BF16),
            jax.ShapeDtypeStruct((rows, KVH * HD), BF16),
            jax.ShapeDtypeStruct((rows, width), F32),
            jax.ShapeDtypeStruct((KVH * HD, width), BF16),
        ),
        input_output_aliases={n: 0, n + 1: 1},
        cost_estimate=pl.CostEstimate(flops=1 << 28, bytes_accessed=1 << 22, transcendentals=0),
        compiler_params=pltpu.CompilerParams(vmem_limit_bytes=28 << 20),
        name="mid",
    )(cut_f, cut_b, *pieces, *state, probs_b, cotangent)


def place_columns(ref, at, depth, value):
    if depth % 128 == 0:
        ref[:, pl.ds(pl.multiple_of(at * depth, 128), depth)] = value
        return
    low = depth * 2 // 128 * 128 // 2 // 128 * 128
    base = lax.div(at, 2) * (2 * depth)

    @pl.when(lax.rem(at, 2) == 0)
    def _():
        ref.at[:, pl.ds(pl.multiple_of(base, 128), 2 * depth)][:, :depth] = value

    @pl.when(lax.rem(at, 2) == 1)
    def _():
        ref.at[:, pl.ds(pl.multiple_of(base + low, 128), 2 * depth - low)][:, depth - low :] = value


def tail_kernel(items, count, factors, axis, *refs):
    cut_f, cut_b = refs[:2]
    pieces, refs = refs[2 : 2 + count], refs[2 + count :]
    (total_ref, _, half_ref, probs_f, probs_b, key_b, grad_v, turned, queries, u_ref, saved_ref,
     cot_ref, scale_ref, gain_scale, gain_values), refs = refs[:15], refs[15:]
    fwd_ref, back_ref, weight, through, total, grad_q, grad_k = refs
    rows, width = u_ref.shape
    keys = KVH * HD
    groups = GROUP // SIDE
    wide = SIDE * HD

    total[...] = total_ref[...]
    add_pieces(items, factors, axis, cut_f, cut_b, pieces, total, weight)
    for offset, column, pair in items:
        at = grid_place(offset, factors, axis)
        depth = pair * pieces[0].shape[0]
        value = weight[pl.ds(pl.multiple_of(at * depth, 16), depth), column:]
        place_columns(through, at, depth, dot(grad_v[...], value, ((1,), (1,))))
    values = total[:, keys:].astype(BF16)
    across = values[rows:].T
    ones = same_segment(rows)
    held = {}

    def grad_probs(k):
        value = beside(across[k * HD : (k + 1) * HD])
        held[k] = dot(stacked(cot_ref, k), value).astype(BF16).astype(F32)

    def grad_scores(k):
        probs = probs_b[k]
        mean = dot((probs * held[k]).astype(BF16), ones)
        held[k] = (probs * (held[k] - mean) * HD**-0.5).astype(BF16)

    def grad_inputs(k):
        scores = held.pop(k)
        grad_queries = dot(scores, key_b[k]).astype(BF16)
        for g in range(groups):
            at = (k * groups + g) * wide
            grad_q[:, at : at + wide] = grad_queries[g * rows : (g + 1) * rows]
        grad = dot(queries[k], scores)
        part = grad[:HD, :rows]
        for j in range(1, SIDE):
            part = part + grad[j * HD : (j + 1) * HD, j * rows : (j + 1) * rows]
        grad_k[k * HD : (k + 1) * HD, :] = part

    def forward(k):
        mixed = dot(probs_f[k], beside(values[:rows, k * HD : (k + 1) * HD]))
        for g in range(groups):
            at = (k * groups + g) * wide
            fwd_ref[:, at : at + wide] = (
                u_ref[:, at : at + wide].astype(F32) + mixed[g * rows : (g + 1) * rows]
            ).astype(BF16)

    staggered((grad_probs, grad_scores, grad_inputs, forward), KVH)
    grads = grad_k[...].T.astype(BF16)
    step = width // 9
    along = jnp.zeros((rows, 1), F32)
    for c in range(0, width, step):
        at = slice(c, c + step)
        full = dot(grads, turned[:, at]) + through[:, at] + grad_q[:, at].astype(F32)
        full = full.astype(BF16)
        grad_q[:, at] = full
        along = along + jnp.sum(full.astype(F32) * gain_values[:, at], axis=-1, keepdims=True)
    scale = scale_ref[:, :1]
    along = along * (scale * scale * scale) / width
    for c in range(0, width, step):
        at = slice(c, c + step)
        grad = grad_q[:, at].astype(F32) * gain_scale[:, at] - saved_ref[:, at].astype(F32) * along
        back_ref[:, at] = cot_ref[:, at] + grad.astype(BF16)


def tail_call(cut_f, cut_b, group, factors, axis, state, through, *others):
    pieces, items = flat(group)
    rows, width = through.shape
    n = 2 + len(pieces)
    fwd_out, back_out, _, _ = pl.pallas_call(
        functools.partial(tail_kernel, items, len(pieces), factors, axis),
        out_shape=(
            jax.ShapeDtypeStruct((rows, width), BF16),
            jax.ShapeDtypeStruct((rows, width), BF16),
            jax.ShapeDtypeStruct(state[1].shape, BF16),
            jax.ShapeDtypeStruct(through.shape, F32),
        ),
        input_output_aliases={n + 1: 2, n + 2: 3},
        scratch_shapes=[
            pltpu.VMEM(state[0].shape, F32),
            pltpu.VMEM((rows, width), BF16),
            pltpu.VMEM((KVH * HD, rows), F32),
        ],
        cost_estimate=pl.CostEstimate(flops=1 << 29, bytes_accessed=1 << 23, transcendentals=0),
        compiler_params=pltpu.CompilerParams(vmem_limit_bytes=30 << 20),
        name="tail",
    )(cut_f, cut_b, *pieces, *state, through, *others)
    return fwd_out, back_out


def shifted(x, axis, factors, steps):
    n = lax.axis_size(axis)
    pairs = []
    for me in range(n):
        source, stride = 0, 1
        for size, step in zip(reversed(factors), reversed(steps)):
            source = source + (me // stride % size + step) % size * stride
            stride = stride * size
        pairs.append((source, me))
    return lax.ppermute(x, axis, pairs)


def grid_factors(mesh, axis):
    n = mesh.shape[axis]
    place = list(mesh.axis_names).index(axis)
    devices = mesh.devices
    line = devices[tuple(slice(None) if i == place else 0 for i in range(devices.ndim))]
    spots = [(*getattr(d, "coords", (i,)), getattr(d, "core_on_chip", 0)) for i, d in enumerate(line)]
    factors, stride = [], 1
    while stride < n:
        moved = [i for i in range(len(spots[0])) if spots[stride][i] != spots[0][i]][0]
        size = len({s[moved] for s in spots[::stride]})
        factors.insert(0, size)
        stride *= size
    return tuple(factors)


def on_device(factors, fwd_prev, saved, back_prev, fwd_docs, back_docs, gain, weight):
    sections = lax.axis_size("section")
    own = weight[0]
    ring = lambda x, by: lax.ppermute(x, "section", [(i, (i + by) % sections) for i in range(sections)])

    def move(x, *steps):
        return shifted(x, "fsdp", factors, steps)

    half = own.shape[1] // 2
    keys = lambda x: x[:, :half]
    values = lambda x: x[:, half:]
    if relayed(factors):
        y0 = move(own, 0, 1, 0)
        z1 = move(own, 1, 0, 0)
        own_k, own_v = keys(own), values(own)
        z3k = move(own_k, 3, 0, 0)
        incoming = ring(fwd_prev[0], 1)
        cotangent = ring(back_prev[0], -1)
        c0 = move(own, 0, 0, 1)
        y1 = move(z1, 0, 1, 0)
        z2k = move(keys(z1), 1, 0, 0)
        z2v = move(values(z1), 1, 0, 0)
        z3v = move(own_v, 3, 0, 0)
        z3yv = move(values(y0), 3, 0, 0)
        y3k = move(z3k, 0, 1, 0)
        y2k = move(z2k, 0, 1, 0)
        y2v = move(z2v, 0, 1, 0)

        def both(x, z, y, column=0):
            return ([x, move(x, 0, 0, 1)], (z, y), column)

        groups = [
            ("keyval", [([own, c0], (0, 0), 0), both(y0, 0, 1), both(z1, 1, 0)]),
            ("keyval", [both(z3k, 3, 0), both(y1, 1, 1), both(z2k, 2, 0)]),
            ("probs", [both(y3k, 3, 1), both(y2k, 2, 1)]),
            ("mid", [both(z2v, 2, 0, half), both(z3v, 3, 0, half)]),
            ("tail", [both(z3yv, 3, 1, half), both(y2v, 2, 1, half)]),
        ]
        parts, grid, axis = factors[0] * factors[1], factors, "fsdp"
    else:
        incoming = ring(fwd_prev[0], 1)
        cotangent = ring(back_prev[0], -1)
        full = lax.all_gather(own, "fsdp", axis=0, tiled=True)
        first, second, third, fourth = jnp.split(full, 4)
        groups = [
            ("keyval", [([first], (0,), 0), ([second], (1,), 0), ([keys(third)], (2,), 0)]),
            ("probs", [([keys(fourth)], (3,), 0)]),
            ("mid", [([values(third)], (2,), half)]),
            ("tail", [([values(fourth)], (3,), half)]),
        ]
        parts, grid, axis = 4, (4,), None
    hid_b, cut_b, scale_b, gain_scale, gain_values, turned_b = norm_call(saved[0], gain, parts, True)
    hid_f, cut_f = norm_call(incoming, gain, parts, False)
    state = None
    for kind, group in groups[:-1]:
        if kind == "probs":
            *state, probs_f, probs_b, key_b = probs_call(
                cut_f, cut_b, group, grid, axis, state, hid_f, hid_b, (fwd_docs, back_docs)
            )
        elif kind == "mid":
            *state, grad_v, through, turned = mid_call(
                cut_f, cut_b, group, grid, axis, state, probs_b, cotangent
            )
        else:
            state = keyval_call(
                cut_f, cut_b, group, grid, axis, state, (saved.shape[2], own.shape[1])
            )
    fwd_out, back_out = tail_call(
        cut_f, cut_b, groups[-1][1], grid, axis, state, through, probs_f, probs_b, key_b, grad_v,
        turned, turned_b, incoming, saved[0], cotangent, scale_b, gain_scale, gain_values,
    )
    return (fwd_out[None], back_out[None])


def relayed(factors):
    return len(factors) == 3 and factors[0] == 4 and factors[1:] == (2, 2)


def solution(mesh):
    in_specs = (
        P("section", "fsdp", None),
        P("section", "fsdp", None),
        P("section", "fsdp", None),
        P("section", "fsdp"),
        P("section", "fsdp"),
        P("section", None),
        P("section", "fsdp", None),
    )
    out_specs = (P("section", "fsdp", None), P("section", "fsdp", None))
    factors = grid_factors(mesh, "fsdp")
    return jax.shard_map(
        functools.partial(on_device, factors),
        mesh=mesh, in_specs=in_specs, out_specs=out_specs, check_vma=False,
    )
```

```python
import functools

import jax
import jax.numpy as jnp
from jax import lax
from jax.experimental import pallas as pl
from jax.experimental.pallas import tpu as pltpu
from jax.sharding import PartitionSpec as P


HD = 96
KVH = 4
GROUP = 12
SIDE = 4
EPSILON = 1e-05
BLOCKS = 2

F32 = jnp.float32
BF16 = jnp.bfloat16


def dot(a, b, over=((1,), (0,))):
    return lax.dot_general(a, b, (over, ((), ())), preferred_element_type=F32)


def norm_kernel(u_ref, gain_ref, hidden_ref, cut_ref, *extra):
    rows, width = u_ref.shape
    parts, _, depth = cut_ref.shape
    step = width // 9
    total = jnp.zeros((rows, 1), F32)
    for c in range(0, width, step):
        values = u_ref[:, c : c + step].astype(F32)
        total = total + jnp.sum(values * values, axis=-1, keepdims=True)
    scale = lax.rsqrt(total / width + EPSILON)
    for c in range(0, width, step):
        at = slice(c, c + step)
        values = u_ref[:, at].astype(F32)
        hidden_ref[:, at] = (values * scale * gain_ref[:, at]).astype(BF16)
    for p in range(parts):
        cut_ref[p] = hidden_ref[:, p * depth : (p + 1) * depth]
    if extra:
        scale_ref, gain_scale, gain_values, turned = extra
        scale_ref[...] = jnp.broadcast_to(scale, scale_ref.shape)
        for c in range(0, width, step):
            at = slice(c, c + step)
            gain_scale[:, at] = gain_ref[:, at] * scale
            gain_values[:, at] = gain_ref[:, at] * u_ref[:, at].astype(F32)
        for k in range(KVH):
            turned[k] = stacked(hidden_ref, k).T


def norm_call(rows_in, gain, parts, backward):
    rows, width = rows_in.shape
    out = [
        jax.ShapeDtypeStruct((rows, width), BF16),
        jax.ShapeDtypeStruct((parts, rows, width // parts), BF16),
    ]
    if backward:
        out += [
            jax.ShapeDtypeStruct((rows, 128), F32),
            jax.ShapeDtypeStruct((rows, width), F32),
            jax.ShapeDtypeStruct((rows, width), F32),
            jax.ShapeDtypeStruct((KVH, SIDE * HD, GROUP // SIDE * rows), BF16),
        ]
    return pl.pallas_call(
        norm_kernel,
        out_shape=out,
        cost_estimate=pl.CostEstimate(
            flops=6 * rows * width, bytes_accessed=6 * rows * width, transcendentals=rows
        ),
        compiler_params=pltpu.CompilerParams(vmem_limit_bytes=12 << 20),
        name="norm",
    )(rows_in, gain)


def grid_place(offset, factors, axis):
    me = 0 if axis is None else lax.axis_index(axis)
    index, stride = 0, 1
    beyond = 1
    for size in factors[len(offset) :]:
        beyond = beyond * size
    for size, away in zip(reversed(factors[: len(offset)]), reversed(offset)):
        mine = lax.rem(lax.div(me, beyond * stride), size)
        index = index + lax.rem(mine + away, size) * stride
        stride = stride * size
    return index


def add_pieces(items, factors, axis, cut_f, cut_b, pieces, total, weight):
    pieces = list(pieces)
    for offset, column, count in items:
        at = grid_place(offset, factors, axis)
        mine = lax.rem(lax.axis_index(axis), count) if count > 1 else 0
        depth, width = pieces[0].shape
        columns = slice(column, column + width)
        start = pl.multiple_of(at * (count * depth), 16)
        for i in range(count):
            row = start + lax.rem(mine + i, count) * depth
            weight[pl.ds(pl.multiple_of(row, 16), depth), columns] = pieces.pop(0)[...]
        value = weight[pl.ds(start, count * depth), columns]
        total[:, columns] += dot(jnp.concatenate([cut_f[at], cut_b[at]], axis=0), value)


def flat(group):
    return [p for item in group for p in item[0]], [(o, c, len(p)) for p, o, c in group]


def keyval_kernel(items, count, factors, axis, first, *refs):
    cut_f, cut_b = refs[:2]
    pieces, (total, weight) = refs[2 : 2 + count], refs[-2:]
    total[...] = jnp.zeros_like(total) if first else refs[2 + count][...]
    add_pieces(items, factors, axis, cut_f, cut_b, pieces, total, weight)


def keyval_call(cut_f, cut_b, group, factors, axis, state, shape):
    pieces, items = flat(group)
    rows = 2 * cut_f.shape[1]
    work = rows * sum(p.size for p in pieces)
    n = 2 + len(pieces)
    return pl.pallas_call(
        functools.partial(keyval_kernel, items, len(pieces), factors, axis, state is None),
        out_shape=(
            jax.ShapeDtypeStruct((rows, shape[1]), F32),
            jax.ShapeDtypeStruct(shape, BF16),
        ),
        input_output_aliases={} if state is None else {n: 0, n + 1: 1},
        cost_estimate=pl.CostEstimate(
            flops=2 * work, bytes_accessed=work // rows * 2, transcendentals=0
        ),
        compiler_params=pltpu.CompilerParams(vmem_limit_bytes=12 << 20),
        name="keyval",
    )(cut_f, cut_b, *pieces, *(() if state is None else state))


def beside(x):
    _, width = x.shape
    wide = jnp.concatenate([x] * SIDE, axis=1)
    lane = lax.broadcasted_iota(jnp.int32, wide.shape, 1)
    blocks = [
        jnp.where((lane >= j * width) & (lane < (j + 1) * width), wide, jnp.zeros_like(wide))
        for j in range(SIDE)
    ]
    return jnp.concatenate(blocks, axis=0)


def diagonal(x, rows, width):
    total = x[:rows, :width]
    for j in range(1, SIDE):
        total = total + x[j * rows : (j + 1) * rows, j * width : (j + 1) * width]
    return total


def same_segment(rows):
    size = SIDE * rows
    a = lax.broadcasted_iota(jnp.int32, (size, size), 0) // rows
    b = lax.broadcasted_iota(jnp.int32, (size, size), 1) // rows
    return (a == b).astype(F32).astype(BF16)


def segment_sum(x, ones):
    high = x.astype(BF16)
    low = (x - high.astype(F32)).astype(BF16)
    return dot(high, ones) + dot(low, ones)


def segment_max(x, rows):
    tiles = []
    for start in range(0, x.shape[1], 128):
        tile = x[:, start : start + 128]
        lane = lax.broadcasted_iota(jnp.int32, tile.shape, 1)
        top = None
        for low in range(0, 128, rows):
            inside = (lane >= low) & (lane < low + rows)
            part = jnp.max(jnp.where(inside, tile, -3e38), axis=-1, keepdims=True)
            top = jnp.broadcast_to(part, tile.shape) if top is None else jnp.where(lane >= low, part, top)
        tiles.append(top)
    return jnp.concatenate(tiles, axis=1)


def staggered(stages, count):
    for step in range(count + len(stages) - 1):
        for i, stage in enumerate(stages):
            if 0 <= step - i < count:
                stage(step - i)


def allowed_mask(docs_ref):
    rows = docs_ref.shape[1]
    row = lax.broadcasted_iota(jnp.int32, (rows, rows), 0)
    col = lax.broadcasted_iota(jnp.int32, (rows, rows), 1)
    across = jnp.broadcast_to(docs_ref[...].astype(F32), (rows, rows))
    down = jnp.sum(jnp.where(row == col, across, 0.0), axis=1, keepdims=True)
    allowed = jnp.where((across == down) & (col <= row), 1.0, 0.0)
    allowed = jnp.concatenate([allowed] * SIDE, axis=1)
    return jnp.concatenate([allowed] * (GROUP // SIDE), axis=0) > 0.5


def stacked(ref, k):
    wide = SIDE * HD
    groups = GROUP // SIDE
    return jnp.concatenate(
        [ref[:, (k * groups + g) * wide : (k * groups + g + 1) * wide] for g in range(groups)], axis=0
    )


def place_columns(ref, at, depth, value):
    if depth % 128 == 0:
        ref[:, pl.ds(pl.multiple_of(at * depth, 128), depth)] = value
        return
    span = pl.ds(pl.multiple_of(lax.div(at, 2) * (2 * depth), 128), 2 * depth)
    old = ref[:, span]
    low = jnp.concatenate([value, old[:, depth:]], axis=1)
    high = jnp.concatenate([old[:, :depth], value], axis=1)
    ref[:, span] = jnp.where(lax.rem(at, 2) == 1, high, low)


def turn_kernel(items, count, factors, axis, *refs):
    cut_f, cut_b = refs[:2]
    pieces, refs = refs[2 : 2 + count], refs[2 + count :]
    old, _, total, weight, turned = refs
    total[...] = old[...]
    add_pieces(items, factors, axis, cut_f, cut_b, pieces, total, weight)
    step = weight.shape[0] // 9
    for c in range(0, weight.shape[0], step):
        turned[:, c : c + step] = weight[c : c + step, :].T


def turn_pieces(items, count, factors, axis, weight, turned):
    for offset, column, pair in items:
        at = grid_place(offset, factors, axis)
        depth = weight.shape[0] // count
        columns = slice(column, column + KVH * HD)
        value = weight[pl.ds(pl.multiple_of(at * depth, 16), depth), columns]
        place_columns(turned.at[columns, :], at, depth, value.T)


def turn_call(cut_f, cut_b, group, factors, axis, state):
    pieces, items = flat(group)
    n = 2 + len(pieces)
    shape = state[1].shape
    return pl.pallas_call(
        functools.partial(turn_kernel, items, len(pieces), factors, axis),
        out_shape=(
            jax.ShapeDtypeStruct(state[0].shape, F32),
            jax.ShapeDtypeStruct(shape, BF16),
            jax.ShapeDtypeStruct(shape[::-1], BF16),
        ),
        input_output_aliases={n: 0, n + 1: 1},
        cost_estimate=pl.CostEstimate(
            flops=1 << 27, bytes_accessed=2 * shape[0] * shape[1], transcendentals=0
        ),
        compiler_params=pltpu.CompilerParams(vmem_limit_bytes=12 << 20),
        name="turn",
    )(cut_f, cut_b, *pieces, *state)


def probs_kernel(items, count, factors, axis, *refs):
    cut_f, cut_b = refs[:2]
    pieces, refs = refs[2 : 2 + count], refs[2 + count :]
    (old, _, _, hid_f, hid_b, docs_f, docs_b,
     total, weight, turned, probs_f, probs_b, key_b) = refs
    rows = hid_f.shape[0]
    total[...] = old[...]
    add_pieces(items, factors, axis, cut_f, cut_b, pieces, total, weight)
    turn_pieces(items, cut_f.shape[0], factors, axis, weight, turned)
    keys = total[:, : KVH * HD].astype(BF16)
    across = keys.T
    ones = same_segment(rows)
    masks = (allowed_mask(docs_f), allowed_mask(docs_b))
    held = {}

    def score(n):
        k, back = n // 2, 1 - n % 2
        key = beside(across[k * HD : (k + 1) * HD, back * rows : (back + 1) * rows])
        held[n] = dot(stacked((hid_f, hid_b)[back], k), key) * HD**-0.5
        if back:
            key_b[k] = beside(keys[rows:, k * HD : (k + 1) * HD])

    def power(n):
        scores = jnp.where(masks[1 - n % 2], held[n], -1e30)
        held[n] = jnp.exp(scores - segment_max(scores, rows))

    def divide(n):
        powers = held.pop(n)
        probs = powers * (1.0 / segment_sum(powers, ones))
        if n % 2 == 0:
            probs_b[n // 2] = probs
        else:
            probs_f[n // 2] = probs.astype(BF16)

    staggered((score, power, divide), 2 * KVH)


def probs_call(cut_f, cut_b, group, factors, axis, state, turned, hid_f, hid_b, docs):
    pieces, items = flat(group)
    rows = hid_f.shape[0]
    n = 2 + len(pieces)
    scores = (KVH, GROUP // SIDE * rows, SIDE * rows)
    return pl.pallas_call(
        functools.partial(probs_kernel, items, len(pieces), factors, axis),
        out_shape=(
            jax.ShapeDtypeStruct(state[0].shape, F32),
            jax.ShapeDtypeStruct(state[1].shape, BF16),
            jax.ShapeDtypeStruct(turned.shape, BF16),
            jax.ShapeDtypeStruct(scores, BF16),
            jax.ShapeDtypeStruct(scores, F32),
            jax.ShapeDtypeStruct((KVH, SIDE * rows, SIDE * HD), BF16),
        ),
        input_output_aliases={n: 0, n + 1: 1, n + 2: 2},
        cost_estimate=pl.CostEstimate(flops=1 << 28, bytes_accessed=1 << 22, transcendentals=1 << 19),
        compiler_params=pltpu.CompilerParams(vmem_limit_bytes=12 << 20),
        name="probs",
    )(cut_f, cut_b, *pieces, *state, turned, hid_f, hid_b, *docs)


def mid_kernel(items, count, factors, axis, *refs):
    cut_f, cut_b = refs[:2]
    pieces, refs = refs[2 : 2 + count], refs[2 + count :]
    old, _, _, probs_b, cot_ref, total, weight, turned, grad_v, through = refs
    rows = cot_ref.shape[0]
    keys = KVH * HD
    depth = weight.shape[0]
    step = depth // 9
    total[...] = old[...]
    add_pieces(items, factors, axis, cut_f, cut_b, pieces, total, weight)
    for k in range(KVH):
        grad = dot(probs_b[k].astype(BF16), stacked(cot_ref, k), ((0,), (0,)))
        grad_v[:, k * HD : (k + 1) * HD] = diagonal(grad, rows, HD).astype(BF16)
    turn_pieces(items, cut_f.shape[0], factors, axis, weight, turned)
    grads = grad_v[...]
    for c in range(0, depth, step):
        at = slice(c, c + step)
        through[:, at] = dot(grads, turned[keys:, at])


def mid_call(cut_f, cut_b, group, factors, axis, state, turned, probs_b, cotangent):
    pieces, items = flat(group)
    rows, width = cotangent.shape
    n = 2 + len(pieces)
    return pl.pallas_call(
        functools.partial(mid_kernel, items, len(pieces), factors, axis),
        out_shape=(
            jax.ShapeDtypeStruct(state[0].shape, F32),
            jax.ShapeDtypeStruct(state[1].shape, BF16),
            jax.ShapeDtypeStruct(turned.shape, BF16),
            jax.ShapeDtypeStruct((rows, KVH * HD), BF16),
            jax.ShapeDtypeStruct((rows, width), F32),
        ),
        input_output_aliases={n: 0, n + 1: 1, n + 2: 2},
        cost_estimate=pl.CostEstimate(flops=1 << 28, bytes_accessed=1 << 22, transcendentals=0),
        compiler_params=pltpu.CompilerParams(vmem_limit_bytes=12 << 20),
        name="mid",
    )(cut_f, cut_b, *pieces, *state, turned, probs_b, cotangent)


def last_values(items, factors, axis, cut_f, cut_b, pieces, grad_v):
    pieces, total, late = list(pieces), 0.0, []
    for offset, column, count in items:
        at = grid_place(offset, factors, axis)
        depth = pieces[0].shape[0]
        left = jnp.concatenate([cut_f[at], cut_b[at]], axis=0)
        values = [pieces.pop(0)[...] for _ in range(count)]
        lefts = [left[:, i * depth : (i + 1) * depth] for i in range(count)]
        parts = [dot(grad_v, value.T) for value in values]
        if count == 2:
            second = lax.rem(lax.axis_index(axis), 2) == 1
            lefts = [jnp.where(second, lefts[1 - i], lefts[i]) for i in range(2)]
            parts = [jnp.where(second, parts[1 - i], parts[i]) for i in range(2)]
        for mine, value in zip(lefts, values):
            total = total + dot(mine, value)
        late.append((at, count * depth, jnp.concatenate(parts, axis=1)))
    return total, late


def tail_kernel(items, count, factors, axis, *refs):
    cut_f, cut_b = refs[:2]
    pieces, refs = refs[2 : 2 + count], refs[2 + count :]
    (total_ref, half_ref, probs_f, probs_b, key_b, grad_v, turned, queries, u_ref, saved_ref,
     cot_ref, scale_ref, gain_scale, gain_values), refs = refs[:14], refs[14:]
    fwd_out, back_out, through, fwd_ref, back_ref, grad_q, grad_k, sems = refs
    rows, width = u_ref.shape
    keys = KVH * HD
    groups = GROUP // SIDE
    wide = SIDE * HD
    copies = []

    def send(source, target, at):
        copies.append(pltpu.make_async_copy(source.at[at], target.at[at], sems.at[len(copies)]))
        copies[-1].start()

    total, late = last_values(items, factors, axis, cut_f, cut_b, pieces, grad_v[...])
    total = total_ref[:, keys:] + total
    values = total.astype(BF16)
    across = values[rows:].T
    ones = same_segment(rows)
    held = {}

    def grad_probs(k):
        value = beside(across[k * HD : (k + 1) * HD])
        held[k] = dot(stacked(cot_ref, k), value).astype(BF16).astype(F32)

    def grad_scores(k):
        probs = probs_b[k]
        mean = dot((probs * held[k]).astype(BF16), ones)
        held[k] = (probs * (held[k] - mean) * HD**-0.5).astype(BF16)

    def grad_inputs(k):
        scores = held.pop(k)
        grad_queries = dot(scores, key_b[k]).astype(BF16)
        for g in range(groups):
            at = (k * groups + g) * wide
            grad_q[:, at : at + wide] = grad_queries[g * rows : (g + 1) * rows]
        grad = dot(queries[k], scores)
        part = grad[:HD, :rows]
        for j in range(1, SIDE):
            part = part + grad[j * HD : (j + 1) * HD, j * rows : (j + 1) * rows]
        grad_k[k * HD : (k + 1) * HD, :] = part

    def forward(k):
        mixed = dot(probs_f[k], beside(values[:rows, k * HD : (k + 1) * HD]))
        for g in range(groups):
            at = (k * groups + g) * wide
            fwd_ref[:, at : at + wide] = (
                u_ref[:, at : at + wide].astype(F32) + mixed[g * rows : (g + 1) * rows]
            ).astype(BF16)

    staggered((grad_probs, grad_scores, grad_inputs, forward), KVH)
    send(fwd_ref, fwd_out, slice(0, rows))
    for at, depth, value in late:
        place_columns(through, at, depth, value)
    grads = grad_k[...].T.astype(BF16)
    step = width // 9
    along = jnp.zeros((rows, 1), F32)
    for c in range(0, width, step):
        at = slice(c, c + step)
        full = dot(grads, turned[:keys, at]) + through[:, at] + grad_q[:, at].astype(F32)
        full = full.astype(BF16).astype(F32)
        through[:, at] = full
        along = along + jnp.sum(full * gain_values[:, at], axis=-1, keepdims=True)
    scale = scale_ref[:, :1]
    along = along * (scale * scale * scale) / width
    block = rows // BLOCKS
    for low in range(0, rows, block):
        lines = slice(low, low + block)
        for c in range(0, width, step):
            at = (lines, slice(c, c + step))
            grad = through[at] * gain_scale[at] - saved_ref[at].astype(F32) * along[lines]
            back_ref[at] = cot_ref[at] + grad.astype(BF16)
        send(back_ref, back_out, lines)
    for copy in copies:
        copy.wait()


def tail_call(cut_f, cut_b, group, factors, axis, total, through, *others):
    pieces, items = flat(group)
    rows, width = through.shape
    vmem, hbm = pl.BlockSpec(memory_space=pltpu.VMEM), pl.BlockSpec(memory_space=pl.ANY)
    operands = (cut_f, cut_b, *pieces, total, through, *others)
    fwd_out, back_out, _ = pl.pallas_call(
        functools.partial(tail_kernel, items, len(pieces), factors, axis),
        out_shape=(
            jax.ShapeDtypeStruct((rows, width), BF16),
            jax.ShapeDtypeStruct((rows, width), BF16),
            jax.ShapeDtypeStruct(through.shape, F32),
        ),
        in_specs=[vmem] * len(operands),
        out_specs=(hbm, hbm, vmem),
        input_output_aliases={3 + len(pieces): 2},
        scratch_shapes=[
            pltpu.VMEM((rows, width), BF16),
            pltpu.VMEM((rows, width), BF16),
            pltpu.VMEM((rows, width), BF16),
            pltpu.VMEM((KVH * HD, rows), F32),
            pltpu.SemaphoreType.DMA((1 + BLOCKS,)),
        ],
        cost_estimate=pl.CostEstimate(flops=1 << 29, bytes_accessed=1 << 23, transcendentals=0),
        compiler_params=pltpu.CompilerParams(vmem_limit_bytes=12 << 20),
        name="tail",
    )(*operands)
    return fwd_out, back_out


def shifted(x, axis, factors, steps):
    n = lax.axis_size(axis)
    pairs = []
    for me in range(n):
        source, stride = 0, 1
        for size, step in zip(reversed(factors), reversed(steps)):
            source = source + (me // stride % size + step) % size * stride
            stride = stride * size
        pairs.append((source, me))
    return lax.ppermute(x, axis, pairs)


def grid_factors(mesh, axis):
    n = mesh.shape[axis]
    place = list(mesh.axis_names).index(axis)
    devices = mesh.devices
    line = devices[tuple(slice(None) if i == place else 0 for i in range(devices.ndim))]
    spots = [(*getattr(d, "coords", (i,)), getattr(d, "core_on_chip", 0)) for i, d in enumerate(line)]
    factors, stride = [], 1
    while stride < n:
        moved = [i for i in range(len(spots[0])) if spots[stride][i] != spots[0][i]][0]
        size = len({s[moved] for s in spots[::stride]})
        factors.insert(0, size)
        stride *= size
    return tuple(factors)


def on_device(factors, fwd_prev, saved, back_prev, fwd_docs, back_docs, gain, weight):
    sections = lax.axis_size("section")
    own = weight[0]
    ring = lambda x, by: lax.ppermute(x, "section", [(i, (i + by) % sections) for i in range(sections)])

    def move(x, *steps):
        return shifted(x, "fsdp", factors, steps)

    half = own.shape[1] // 2
    keys = lambda x: x[:, :half]
    values = lambda x: x[:, half:]
    if relayed(factors):
        y0 = move(own, 0, 1, 0)
        z1 = move(own, 1, 0, 0)
        own_k, own_v = keys(own), values(own)
        z3k = move(own_k, 3, 0, 0)
        incoming = ring(fwd_prev[0], 1)
        cotangent = ring(back_prev[0], -1)
        c0 = move(own, 0, 0, 1)
        y1 = move(z1, 0, 1, 0)
        z2k = move(keys(z1), 1, 0, 0)
        z2v = move(values(z1), 1, 0, 0)
        z3v = move(own_v, 3, 0, 0)
        z3yv = move(values(y0), 3, 0, 0)
        y3k = move(z3k, 0, 1, 0)
        y2k = move(z2k, 0, 1, 0)
        y2v = move(z2v, 0, 1, 0)

        def both(x, z, y, column=0):
            return ([x, move(x, 0, 0, 1)], (z, y), column)

        groups = [
            ("keyval", [([own, c0], (0, 0), 0), both(y0, 0, 1), both(z1, 1, 0)]),
            ("keyval", [both(z3k, 3, 0), both(y1, 1, 1), both(z2k, 2, 0)]),
            ("turn", [both(z2v, 2, 0, half)]),
            ("probs", [both(y3k, 3, 1), both(y2k, 2, 1)]),
            ("mid", [both(z3v, 3, 0, half)]),
            ("tail", [both(z3yv, 3, 1, half), both(y2v, 2, 1, half)]),
        ]
        parts, grid, axis = factors[0] * factors[1], factors, "fsdp"
    else:
        incoming = ring(fwd_prev[0], 1)
        cotangent = ring(back_prev[0], -1)
        full = lax.all_gather(own, "fsdp", axis=0, tiled=True)
        first, second, third, fourth = jnp.split(full, 4)
        groups = [
            ("keyval", [([first], (0,), 0), ([second], (1,), 0)]),
            ("turn", [([keys(third)], (2,), 0)]),
            ("probs", [([keys(fourth)], (3,), 0)]),
            ("mid", [([values(third)], (2,), half)]),
            ("tail", [([values(fourth)], (3,), half)]),
        ]
        parts, grid, axis = 4, (4,), None
    hid_b, cut_b, scale_b, gain_scale, gain_values, turned_b = norm_call(saved[0], gain, parts, True)
    hid_f, cut_f = norm_call(incoming, gain, parts, False)
    state, turned = None, None
    for kind, group in groups[:-1]:
        if kind == "turn":
            *state, turned = turn_call(cut_f, cut_b, group, grid, axis, state)
        elif kind == "probs":
            *state, turned, probs_f, probs_b, key_b = probs_call(
                cut_f, cut_b, group, grid, axis, state, turned, hid_f, hid_b,
                (fwd_docs, back_docs),
            )
        elif kind == "mid":
            *state, turned, grad_v, through = mid_call(
                cut_f, cut_b, group, grid, axis, state, turned, probs_b, cotangent
            )
        else:
            state = keyval_call(
                cut_f, cut_b, group, grid, axis, state, (saved.shape[2], own.shape[1])
            )
    fwd_out, back_out = tail_call(
        cut_f, cut_b, groups[-1][1], grid, axis, state[0], through, probs_f, probs_b, key_b,
        grad_v, turned, turned_b, incoming, saved[0], cotangent, scale_b, gain_scale, gain_values,
    )
    return (fwd_out[None], back_out[None])


def relayed(factors):
    return len(factors) == 3 and factors[0] == 4 and factors[1:] == (2, 2)


def solution(mesh):
    in_specs = (
        P("section", "fsdp", None),
        P("section", "fsdp", None),
        P("section", "fsdp", None),
        P("section", "fsdp"),
        P("section", "fsdp"),
        P("section", None),
        P("section", "fsdp", None),
    )
    out_specs = (P("section", "fsdp", None), P("section", "fsdp", None))
    factors = grid_factors(mesh, "fsdp")
    return jax.shard_map(
        functools.partial(on_device, factors),
        mesh=mesh, in_specs=in_specs, out_specs=out_specs, check_vma=False,
    )
```

```python
import functools

import jax
import jax.numpy as jnp
from jax import lax
from jax.experimental import pallas as pl
from jax.experimental.pallas import tpu as pltpu
from jax.sharding import PartitionSpec as P


HD = 96
KVH = 4
GROUP = 12
SIDE = 4
EPSILON = 1e-05
BLOCKS = 2

F32 = jnp.float32
BF16 = jnp.bfloat16


def dot(a, b, over=((1,), (0,))):
    return lax.dot_general(a, b, (over, ((), ())), preferred_element_type=F32)


def norm_kernel(u_ref, gain_ref, hidden_ref, cut_ref, fine_ref, *extra):
    rows, width = u_ref.shape
    parts, _, depth = cut_ref.shape
    step = width // 9
    total = jnp.zeros((rows, 1), F32)
    for c in range(0, width, step):
        values = u_ref[:, c : c + step].astype(F32)
        total = total + jnp.sum(values * values, axis=-1, keepdims=True)
    scale = lax.rsqrt(total / width + EPSILON)
    for c in range(0, width, step):
        at = slice(c, c + step)
        values = u_ref[:, at].astype(F32)
        hidden_ref[:, at] = (values * scale * gain_ref[:, at]).astype(BF16)
    for p in range(parts):
        cut_ref[p] = hidden_ref[:, p * depth : (p + 1) * depth]
    pieces, _, depth = fine_ref.shape
    for p in range(pieces):
        fine_ref[p] = hidden_ref[:, p * depth : (p + 1) * depth]
    if extra:
        scale_ref, gain_scale, gain_values, turned = extra
        scale_ref[...] = jnp.broadcast_to(scale, scale_ref.shape)
        for c in range(0, width, step):
            at = slice(c, c + step)
            gain_scale[:, at] = gain_ref[:, at] * scale
            gain_values[:, at] = gain_ref[:, at] * u_ref[:, at].astype(F32)
        for k in range(KVH):
            turned[k] = stacked(hidden_ref, k).T


def norm_call(rows_in, gain, parts, pieces, backward):
    rows, width = rows_in.shape
    out = [
        jax.ShapeDtypeStruct((rows, width), BF16),
        jax.ShapeDtypeStruct((parts, rows, width // parts), BF16),
        jax.ShapeDtypeStruct((pieces, rows, width // pieces), BF16),
    ]
    if backward:
        out += [
            jax.ShapeDtypeStruct((rows, 128), F32),
            jax.ShapeDtypeStruct((rows, width), F32),
            jax.ShapeDtypeStruct((rows, width), F32),
            jax.ShapeDtypeStruct((KVH, SIDE * HD, GROUP // SIDE * rows), BF16),
        ]
    return pl.pallas_call(
        norm_kernel,
        out_shape=out,
        cost_estimate=pl.CostEstimate(
            flops=6 * rows * width, bytes_accessed=6 * rows * width, transcendentals=rows
        ),
        compiler_params=pltpu.CompilerParams(vmem_limit_bytes=12 << 20),
        name="norm",
    )(rows_in, gain)


def grid_place(offset, factors, axis):
    me = 0 if axis is None else lax.axis_index(axis)
    index, stride = 0, 1
    beyond = 1
    for size in factors[len(offset) :]:
        beyond = beyond * size
    for size, away in zip(reversed(factors[: len(offset)]), reversed(offset)):
        mine = lax.rem(lax.div(me, beyond * stride), size)
        index = index + lax.rem(mine + away, size) * stride
        stride = stride * size
    return index


def add_pieces(items, factors, axis, cut_f, cut_b, pieces, total, weight):
    pieces = list(pieces)
    for offset, column, count in items:
        at = grid_place(offset, factors, axis)
        mine = lax.rem(lax.axis_index(axis), count) if count > 1 else 0
        depth, width = pieces[0].shape
        columns = slice(column, column + width)
        start = pl.multiple_of(at * (count * depth), 16)
        for i in range(count):
            row = start + lax.rem(mine + i, count) * depth
            weight[pl.ds(pl.multiple_of(row, 16), depth), columns] = pieces.pop(0)[...]
        value = weight[pl.ds(start, count * depth), columns]
        total[:, columns] += dot(jnp.concatenate([cut_f[at], cut_b[at]], axis=0), value)


def flat(group):
    return [p for item in group for p in item[0]], [(o, c, len(p)) for p, o, c in group]


def keyval_kernel(items, count, factors, axis, first, *refs):
    cut_f, cut_b = refs[:2]
    pieces, (total, weight) = refs[2 : 2 + count], refs[-2:]
    total[...] = jnp.zeros_like(total) if first else refs[2 + count][...]
    add_pieces(items, factors, axis, cut_f, cut_b, pieces, total, weight)


def keyval_call(cut_f, cut_b, group, factors, axis, state, shape):
    pieces, items = flat(group)
    rows = 2 * cut_f.shape[1]
    work = rows * sum(p.size for p in pieces)
    n = 2 + len(pieces)
    return pl.pallas_call(
        functools.partial(keyval_kernel, items, len(pieces), factors, axis, state is None),
        out_shape=(
            jax.ShapeDtypeStruct((rows, shape[1]), F32),
            jax.ShapeDtypeStruct(shape, BF16),
        ),
        input_output_aliases={} if state is None else {n: 0, n + 1: 1},
        cost_estimate=pl.CostEstimate(
            flops=2 * work, bytes_accessed=work // rows * 2, transcendentals=0
        ),
        compiler_params=pltpu.CompilerParams(vmem_limit_bytes=12 << 20),
        name="keyval",
    )(cut_f, cut_b, *pieces, *(() if state is None else state))


def beside(x):
    _, width = x.shape
    wide = jnp.concatenate([x] * SIDE, axis=1)
    lane = lax.broadcasted_iota(jnp.int32, wide.shape, 1)
    blocks = [
        jnp.where((lane >= j * width) & (lane < (j + 1) * width), wide, jnp.zeros_like(wide))
        for j in range(SIDE)
    ]
    return jnp.concatenate(blocks, axis=0)


def diagonal(x, rows, width):
    total = x[:rows, :width]
    for j in range(1, SIDE):
        total = total + x[j * rows : (j + 1) * rows, j * width : (j + 1) * width]
    return total


def same_segment(rows):
    size = SIDE * rows
    a = lax.broadcasted_iota(jnp.int32, (size, size), 0) // rows
    b = lax.broadcasted_iota(jnp.int32, (size, size), 1) // rows
    return (a == b).astype(F32).astype(BF16)


def segment_sum(x, ones):
    high = x.astype(BF16)
    low = (x - high.astype(F32)).astype(BF16)
    return dot(high, ones) + dot(low, ones)


def segment_max(x, rows):
    tiles = []
    for start in range(0, x.shape[1], 128):
        tile = x[:, start : start + 128]
        lane = lax.broadcasted_iota(jnp.int32, tile.shape, 1)
        top = None
        for low in range(0, 128, rows):
            inside = (lane >= low) & (lane < low + rows)
            part = jnp.max(jnp.where(inside, tile, -3e38), axis=-1, keepdims=True)
            top = jnp.broadcast_to(part, tile.shape) if top is None else jnp.where(lane >= low, part, top)
        tiles.append(top)
    return jnp.concatenate(tiles, axis=1)


def staggered(stages, count):
    for step in range(count + len(stages) - 1):
        for i, stage in enumerate(stages):
            if 0 <= step - i < count:
                stage(step - i)


def allowed_mask(docs_ref):
    rows = docs_ref.shape[1]
    row = lax.broadcasted_iota(jnp.int32, (rows, rows), 0)
    col = lax.broadcasted_iota(jnp.int32, (rows, rows), 1)
    across = jnp.broadcast_to(docs_ref[...].astype(F32), (rows, rows))
    down = jnp.sum(jnp.where(row == col, across, 0.0), axis=1, keepdims=True)
    allowed = jnp.where((across == down) & (col <= row), 1.0, 0.0)
    allowed = jnp.concatenate([allowed] * SIDE, axis=1)
    return jnp.concatenate([allowed] * (GROUP // SIDE), axis=0) > 0.5


def stacked(ref, k):
    wide = SIDE * HD
    groups = GROUP // SIDE
    return jnp.concatenate(
        [ref[:, (k * groups + g) * wide : (k * groups + g + 1) * wide] for g in range(groups)], axis=0
    )


def place_columns(ref, at, depth, value):
    if depth % 128 == 0:
        ref[:, pl.ds(pl.multiple_of(at * depth, 128), depth)] = value
        return
    span = pl.ds(pl.multiple_of(lax.div(at, 2) * (2 * depth), 128), 2 * depth)
    old = ref[:, span]
    low = jnp.concatenate([value, old[:, depth:]], axis=1)
    high = jnp.concatenate([old[:, :depth], value], axis=1)
    ref[:, span] = jnp.where(lax.rem(at, 2) == 1, high, low)


def turn_kernel(items, count, factors, axis, *refs):
    cut_f, cut_b = refs[:2]
    pieces, refs = refs[2 : 2 + count], refs[2 + count :]
    old, _, total, weight, turned = refs
    total[...] = old[...]
    add_pieces(items, factors, axis, cut_f, cut_b, pieces, total, weight)
    step = weight.shape[0] // 9
    for c in range(0, weight.shape[0], step):
        turned[:, c : c + step] = weight[c : c + step, :].T


def turn_pieces(items, count, factors, axis, weight, turned):
    for offset, column, pair in items:
        at = grid_place(offset, factors, axis)
        depth = weight.shape[0] // count
        columns = slice(column, column + KVH * HD)
        value = weight[pl.ds(pl.multiple_of(at * depth, 16), depth), columns]
        place_columns(turned.at[columns, :], at, depth, value.T)


def turn_call(cut_f, cut_b, group, factors, axis, state):
    pieces, items = flat(group)
    n = 2 + len(pieces)
    shape = state[1].shape
    return pl.pallas_call(
        functools.partial(turn_kernel, items, len(pieces), factors, axis),
        out_shape=(
            jax.ShapeDtypeStruct(state[0].shape, F32),
            jax.ShapeDtypeStruct(shape, BF16),
            jax.ShapeDtypeStruct(shape[::-1], BF16),
        ),
        input_output_aliases={n: 0, n + 1: 1},
        cost_estimate=pl.CostEstimate(
            flops=1 << 27, bytes_accessed=2 * shape[0] * shape[1], transcendentals=0
        ),
        compiler_params=pltpu.CompilerParams(vmem_limit_bytes=12 << 20),
        name="turn",
    )(cut_f, cut_b, *pieces, *state)


def probs_kernel(items, count, factors, axis, *refs):
    cut_f, cut_b = refs[:2]
    pieces, refs = refs[2 : 2 + count], refs[2 + count :]
    (old, _, _, hid_f, hid_b, docs_f, docs_b,
     total, weight, turned, probs_f, probs_b, key_b) = refs
    rows = hid_f.shape[0]
    total[...] = old[...]
    add_pieces(items, factors, axis, cut_f, cut_b, pieces, total, weight)
    turn_pieces(items, cut_f.shape[0], factors, axis, weight, turned)
    keys = total[:, : KVH * HD].astype(BF16)
    across = keys.T
    ones = same_segment(rows)
    masks = (allowed_mask(docs_f), allowed_mask(docs_b))
    held = {}

    def score(n):
        k, back = n // 2, 1 - n % 2
        key = beside(across[k * HD : (k + 1) * HD, back * rows : (back + 1) * rows])
        held[n] = dot(stacked((hid_f, hid_b)[back], k), key) * HD**-0.5
        if back:
            key_b[k] = beside(keys[rows:, k * HD : (k + 1) * HD])

    def power(n):
        scores = jnp.where(masks[1 - n % 2], held[n], -1e30)
        held[n] = jnp.exp(scores - segment_max(scores, rows))

    def divide(n):
        powers = held.pop(n)
        probs = powers * (1.0 / segment_sum(powers, ones))
        if n % 2 == 0:
            probs_b[n // 2] = probs
        else:
            probs_f[n // 2] = probs.astype(BF16)

    staggered((score, power, divide), 2 * KVH)


def probs_call(cut_f, cut_b, group, factors, axis, state, turned, hid_f, hid_b, docs):
    pieces, items = flat(group)
    rows = hid_f.shape[0]
    n = 2 + len(pieces)
    scores = (KVH, GROUP // SIDE * rows, SIDE * rows)
    return pl.pallas_call(
        functools.partial(probs_kernel, items, len(pieces), factors, axis),
        out_shape=(
            jax.ShapeDtypeStruct(state[0].shape, F32),
            jax.ShapeDtypeStruct(state[1].shape, BF16),
            jax.ShapeDtypeStruct(turned.shape, BF16),
            jax.ShapeDtypeStruct(scores, BF16),
            jax.ShapeDtypeStruct(scores, F32),
            jax.ShapeDtypeStruct((KVH, SIDE * rows, SIDE * HD), BF16),
        ),
        input_output_aliases={n: 0, n + 1: 1, n + 2: 2},
        cost_estimate=pl.CostEstimate(flops=1 << 28, bytes_accessed=1 << 22, transcendentals=1 << 19),
        compiler_params=pltpu.CompilerParams(vmem_limit_bytes=12 << 20),
        name="probs",
    )(cut_f, cut_b, *pieces, *state, turned, hid_f, hid_b, *docs)


def more_kernel(items, count, factors, axis, *refs):
    cut_f, cut_b = refs[:2]
    pieces, refs = refs[2 : 2 + count], refs[2 + count :]
    old, _, _, total, weight, turned = refs
    total[...] = old[...]
    add_pieces(items, factors, axis, cut_f, cut_b, pieces, total, weight)
    turn_pieces(items, cut_f.shape[0], factors, axis, weight, turned)


def more_call(cut_f, cut_b, group, factors, axis, state, turned):
    pieces, items = flat(group)
    n = 2 + len(pieces)
    return pl.pallas_call(
        functools.partial(more_kernel, items, len(pieces), factors, axis),
        out_shape=(
            jax.ShapeDtypeStruct(state[0].shape, F32),
            jax.ShapeDtypeStruct(state[1].shape, BF16),
            jax.ShapeDtypeStruct(turned.shape, BF16),
        ),
        input_output_aliases={n: 0, n + 1: 1, n + 2: 2},
        cost_estimate=pl.CostEstimate(flops=1 << 26, bytes_accessed=1 << 20, transcendentals=0),
        compiler_params=pltpu.CompilerParams(vmem_limit_bytes=12 << 20),
        name="more",
    )(cut_f, cut_b, *pieces, *state, turned)


def mid_kernel(turned, probs_b, cot_ref, grad_v, through):
    rows, depth = through.shape
    keys = KVH * HD
    step = depth // 9
    for k in range(KVH):
        grad = dot(probs_b[k].astype(BF16), stacked(cot_ref, k), ((0,), (0,)))
        grad_v[:, k * HD : (k + 1) * HD] = diagonal(grad, rows, HD).astype(BF16)
    grads = grad_v[...]
    for c in range(0, depth, step):
        at = slice(c, c + step)
        through[:, at] = dot(grads, turned[keys:, at])


def mid_call(turned, probs_b, cotangent):
    rows, width = cotangent.shape
    return pl.pallas_call(
        mid_kernel,
        out_shape=(
            jax.ShapeDtypeStruct((rows, KVH * HD), BF16),
            jax.ShapeDtypeStruct((rows, width), F32),
        ),
        cost_estimate=pl.CostEstimate(flops=1 << 28, bytes_accessed=1 << 22, transcendentals=0),
        compiler_params=pltpu.CompilerParams(vmem_limit_bytes=12 << 20),
        name="mid",
    )(turned, probs_b, cotangent)


def last_values(items, factors, axis, cut_f, cut_b, pieces, grad_v):
    pieces, total, late = list(pieces), 0.0, []
    for offset, column, count in items:
        at = grid_place(offset, factors, axis)
        depth = pieces[0].shape[0]
        values = [pieces.pop(0)[...] for _ in range(count)]
        mine = lax.rem(lax.axis_index(axis), count) if count > 1 else 0
        order = [at * count + lax.rem(mine + i, count) for i in range(count)]
        lefts = [jnp.concatenate([cut_f[i], cut_b[i]], axis=0) for i in order]
        parts = [dot(grad_v, value.T) for value in values]
        if count == 2:
            second = lax.rem(lax.axis_index(axis), 2) == 1
            parts = [jnp.where(second, parts[1 - i], parts[i]) for i in range(2)]
        for left, value in zip(lefts, values):
            total = total + dot(left, value)
        late.append((at, count * depth, jnp.concatenate(parts, axis=1)))
    return total, late


def tail_kernel(items, count, factors, axis, *refs):
    cut_f, cut_b = refs[:2]
    pieces, refs = refs[2 : 2 + count], refs[2 + count :]
    (total_ref, half_ref, probs_f, probs_b, key_b, grad_v, turned, queries, u_ref, saved_ref,
     cot_ref, scale_ref, gain_scale, gain_values), refs = refs[:14], refs[14:]
    fwd_out, back_out, through, fwd_ref, back_ref, grad_q, grad_k, sems = refs
    rows, width = u_ref.shape
    keys = KVH * HD
    groups = GROUP // SIDE
    wide = SIDE * HD
    copies = []

    def send(source, target, at):
        copies.append(pltpu.make_async_copy(source.at[at], target.at[at], sems.at[len(copies)]))
        copies[-1].start()

    total, late = last_values(items, factors, axis, cut_f, cut_b, pieces, grad_v[...])
    total = total_ref[:, keys:] + total
    for at, depth, value in late:
        place_columns(through, at, depth, value)
    values = total.astype(BF16)
    across = values[rows:].T
    ones = same_segment(rows)
    held = {}

    def grad_probs(k):
        value = beside(across[k * HD : (k + 1) * HD])
        held[k] = dot(stacked(cot_ref, k), value).astype(BF16).astype(F32)

    def grad_scores(k):
        probs = probs_b[k]
        mean = dot((probs * held[k]).astype(BF16), ones)
        held[k] = (probs * (held[k] - mean) * HD**-0.5).astype(BF16)

    def grad_inputs(k):
        scores = held.pop(k)
        grad_queries = dot(scores, key_b[k]).astype(BF16)
        for g in range(groups):
            at = (k * groups + g) * wide
            grad_q[:, at : at + wide] = grad_queries[g * rows : (g + 1) * rows]
        grad = dot(queries[k], scores)
        part = grad[:HD, :rows]
        for j in range(1, SIDE):
            part = part + grad[j * HD : (j + 1) * HD, j * rows : (j + 1) * rows]
        grad_k[k * HD : (k + 1) * HD, :] = part

    def forward(k):
        mixed = dot(probs_f[k], beside(values[:rows, k * HD : (k + 1) * HD]))
        for g in range(groups):
            at = (k * groups + g) * wide
            fwd_ref[:, at : at + wide] = (
                u_ref[:, at : at + wide].astype(F32) + mixed[g * rows : (g + 1) * rows]
            ).astype(BF16)
        if k == KVH - 1:
            send(fwd_ref, fwd_out, slice(0, rows))

    staggered((forward, grad_probs, grad_scores, grad_inputs), KVH)
    grads = grad_k[...].T.astype(BF16)
    step = width // 9
    along = jnp.zeros((rows, 1), F32)
    for c in range(0, width, step):
        at = slice(c, c + step)
        full = dot(grads, turned[:keys, at]) + through[:, at] + grad_q[:, at].astype(F32)
        full = full.astype(BF16).astype(F32)
        through[:, at] = full
        along = along + jnp.sum(full * gain_values[:, at], axis=-1, keepdims=True)
    scale = scale_ref[:, :1]
    along = along * (scale * scale * scale) / width
    block = rows // BLOCKS
    for low in range(0, rows, block):
        lines = slice(low, low + block)
        for c in range(0, width, step):
            at = (lines, slice(c, c + step))
            grad = through[at] * gain_scale[at] - saved_ref[at].astype(F32) * along[lines]
            back_ref[at] = cot_ref[at] + grad.astype(BF16)
        send(back_ref, back_out, lines)
    for copy in copies:
        copy.wait()


def tail_call(cut_f, cut_b, group, factors, axis, total, through, *others):
    pieces, items = flat(group)
    rows, width = through.shape
    vmem, hbm = pl.BlockSpec(memory_space=pltpu.VMEM), pl.BlockSpec(memory_space=pl.ANY)
    operands = (cut_f, cut_b, *pieces, total, through, *others)
    fwd_out, back_out, _ = pl.pallas_call(
        functools.partial(tail_kernel, items, len(pieces), factors, axis),
        out_shape=(
            jax.ShapeDtypeStruct((rows, width), BF16),
            jax.ShapeDtypeStruct((rows, width), BF16),
            jax.ShapeDtypeStruct(through.shape, F32),
        ),
        in_specs=[vmem] * len(operands),
        out_specs=(hbm, hbm, vmem),
        input_output_aliases={3 + len(pieces): 2},
        scratch_shapes=[
            pltpu.VMEM((rows, width), BF16),
            pltpu.VMEM((rows, width), BF16),
            pltpu.VMEM((rows, width), BF16),
            pltpu.VMEM((KVH * HD, rows), F32),
            pltpu.SemaphoreType.DMA((1 + BLOCKS,)),
        ],
        cost_estimate=pl.CostEstimate(flops=1 << 29, bytes_accessed=1 << 23, transcendentals=0),
        compiler_params=pltpu.CompilerParams(vmem_limit_bytes=12 << 20),
        name="tail",
    )(*operands)
    return fwd_out, back_out


def shifted(x, axis, factors, steps):
    n = lax.axis_size(axis)
    pairs = []
    for me in range(n):
        source, stride = 0, 1
        for size, step in zip(reversed(factors), reversed(steps)):
            source = source + (me // stride % size + step) % size * stride
            stride = stride * size
        pairs.append((source, me))
    return lax.ppermute(x, axis, pairs)


def grid_factors(mesh, axis):
    n = mesh.shape[axis]
    place = list(mesh.axis_names).index(axis)
    devices = mesh.devices
    line = devices[tuple(slice(None) if i == place else 0 for i in range(devices.ndim))]
    spots = [(*getattr(d, "coords", (i,)), getattr(d, "core_on_chip", 0)) for i, d in enumerate(line)]
    factors, stride = [], 1
    while stride < n:
        moved = [i for i in range(len(spots[0])) if spots[stride][i] != spots[0][i]][0]
        size = len({s[moved] for s in spots[::stride]})
        factors.insert(0, size)
        stride *= size
    return tuple(factors)


def on_device(factors, fwd_prev, saved, back_prev, fwd_docs, back_docs, gain, weight):
    sections = lax.axis_size("section")
    n = lax.axis_size("fsdp")
    own = weight[0]
    ring = lambda x, by: lax.ppermute(x, "section", [(i, (i + by) % sections) for i in range(sections)])

    def move(x, *steps):
        return shifted(x, "fsdp", factors, steps)

    half = own.shape[1] // 2
    keys = lambda x: x[:, :half]
    values = lambda x: x[:, half:]
    if relayed(factors):
        y0 = move(own, 0, 1, 0)
        z1 = move(own, 1, 0, 0)
        own_k, own_v = keys(own), values(own)
        z3k = move(own_k, 3, 0, 0)
        incoming = ring(fwd_prev[0], 1)
        cotangent = ring(back_prev[0], -1)
        c0 = move(own, 0, 0, 1)
        y1 = move(z1, 0, 1, 0)
        z2k = move(keys(z1), 1, 0, 0)
        z2v = move(values(z1), 1, 0, 0)
        z3v = move(own_v, 3, 0, 0)
        z3yv = move(values(y0), 3, 0, 0)
        y3k = move(z3k, 0, 1, 0)
        y2k = move(z2k, 0, 1, 0)
        y2v = move(z2v, 0, 1, 0)

        def both(x, z, y, column=0):
            return ([x, move(x, 0, 0, 1)], (z, y), column)

        groups = [
            ("keyval", [([own, c0], (0, 0), 0), both(y0, 0, 1), both(z1, 1, 0)]),
            ("keyval", [both(z3k, 3, 0), both(y1, 1, 1), both(z2k, 2, 0)]),
            ("turn", [both(z2v, 2, 0, half), both(y3k, 3, 1)]),
            ("more", [both(z3v, 3, 0, half)]),
            ("probs", [both(y2k, 2, 1)]),
            ("tail", [both(z3yv, 3, 1, half), both(y2v, 2, 1, half)]),
        ]
        parts, pieces, grid, axis = factors[0] * factors[1], n, factors, "fsdp"
    else:
        incoming = ring(fwd_prev[0], 1)
        cotangent = ring(back_prev[0], -1)
        full = lax.all_gather(own, "fsdp", axis=0, tiled=True)
        first, second, third, fourth = jnp.split(full, 4)
        groups = [
            ("keyval", [([first], (0,), 0), ([second], (1,), 0)]),
            ("turn", [([keys(third)], (2,), 0)]),
            ("more", [([values(third)], (2,), half)]),
            ("probs", [([keys(fourth)], (3,), 0)]),
            ("tail", [([values(fourth)], (3,), half)]),
        ]
        parts, pieces, grid, axis = 4, 4, (4,), None
    hid_b, cut_b, fine_b, scale_b, gain_scale, gain_values, turned_b = norm_call(
        saved[0], gain, parts, pieces, True
    )
    hid_f, cut_f, fine_f = norm_call(incoming, gain, parts, pieces, False)
    state, turned = None, None
    for kind, group in groups[:-1]:
        if kind == "turn":
            *state, turned = turn_call(cut_f, cut_b, group, grid, axis, state)
        elif kind == "probs":
            *state, turned, probs_f, probs_b, key_b = probs_call(
                cut_f, cut_b, group, grid, axis, state, turned, hid_f, hid_b,
                (fwd_docs, back_docs),
            )
        elif kind == "more":
            *state, turned = more_call(cut_f, cut_b, group, grid, axis, state, turned)
        else:
            state = keyval_call(
                cut_f, cut_b, group, grid, axis, state, (saved.shape[2], own.shape[1])
            )
    grad_v, through = mid_call(turned, probs_b, cotangent)
    fwd_out, back_out = tail_call(
        fine_f, fine_b, groups[-1][1], grid, axis, state[0], through, probs_f, probs_b, key_b,
        grad_v, turned, turned_b, incoming, saved[0], cotangent, scale_b, gain_scale, gain_values,
    )
    return (fwd_out[None], back_out[None])


def relayed(factors):
    return len(factors) == 3 and factors[0] == 4 and factors[1:] == (2, 2)


def solution(mesh):
    in_specs = (
        P("section", "fsdp", None),
        P("section", "fsdp", None),
        P("section", "fsdp", None),
        P("section", "fsdp"),
        P("section", "fsdp"),
        P("section", None),
        P("section", "fsdp", None),
    )
    out_specs = (P("section", "fsdp", None), P("section", "fsdp", None))
    factors = grid_factors(mesh, "fsdp")
    return jax.shard_map(
        functools.partial(on_device, factors),
        mesh=mesh, in_specs=in_specs, out_specs=out_specs, check_vma=False,
    )
```

```python
import functools

import jax
import jax.numpy as jnp
from jax import lax
from jax.experimental import pallas as pl
from jax.experimental.pallas import tpu as pltpu
from jax.sharding import PartitionSpec as P


HD = 96
KVH = 4
GROUP = 12
SIDE = 4
EPSILON = 1e-05
BLOCKS = 2

F32 = jnp.float32
BF16 = jnp.bfloat16


def dot(a, b, over=((1,), (0,))):
    return lax.dot_general(a, b, (over, ((), ())), preferred_element_type=F32)


def norm_kernel(u_ref, gain_ref, hidden_ref, cut_ref, *extra):
    rows, width = u_ref.shape
    parts, _, depth = cut_ref.shape
    step = width // 9
    total = jnp.zeros((rows, 1), F32)
    for c in range(0, width, step):
        values = u_ref[:, c : c + step].astype(F32)
        total = total + jnp.sum(values * values, axis=-1, keepdims=True)
    scale = lax.rsqrt(total / width + EPSILON)
    for c in range(0, width, step):
        at = slice(c, c + step)
        values = u_ref[:, at].astype(F32)
        hidden_ref[:, at] = (values * scale * gain_ref[:, at]).astype(BF16)
    for p in range(parts):
        cut_ref[p] = hidden_ref[:, p * depth : (p + 1) * depth]
    if extra:
        scale_ref, gain_scale, gain_values, turned = extra
        scale_ref[...] = jnp.broadcast_to(scale, scale_ref.shape)
        for c in range(0, width, step):
            at = slice(c, c + step)
            gain_scale[:, at] = gain_ref[:, at] * scale
            gain_values[:, at] = gain_ref[:, at] * u_ref[:, at].astype(F32)
        for k in range(KVH):
            turned[k] = stacked(hidden_ref, k).T


def norm_call(rows_in, gain, parts, backward):
    rows, width = rows_in.shape
    out = [
        jax.ShapeDtypeStruct((rows, width), BF16),
        jax.ShapeDtypeStruct((parts, rows, width // parts), BF16),
    ]
    if backward:
        out += [
            jax.ShapeDtypeStruct((rows, 128), F32),
            jax.ShapeDtypeStruct((rows, width), F32),
            jax.ShapeDtypeStruct((rows, width), F32),
            jax.ShapeDtypeStruct((KVH, SIDE * HD, GROUP // SIDE * rows), BF16),
        ]
    return pl.pallas_call(
        norm_kernel,
        out_shape=out,
        cost_estimate=pl.CostEstimate(
            flops=6 * rows * width, bytes_accessed=6 * rows * width, transcendentals=rows
        ),
        compiler_params=pltpu.CompilerParams(vmem_limit_bytes=12 << 20),
        name="norm",
    )(rows_in, gain)


def grid_place(offset, factors, axis):
    me = 0 if axis is None else lax.axis_index(axis)
    index, stride = 0, 1
    beyond = 1
    for size in factors[len(offset) :]:
        beyond = beyond * size
    for size, away in zip(reversed(factors[: len(offset)]), reversed(offset)):
        mine = lax.rem(lax.div(me, beyond * stride), size)
        index = index + lax.rem(mine + away, size) * stride
        stride = stride * size
    return index


def add_pieces(items, factors, axis, cut_f, cut_b, pieces, total, weight):
    pieces = list(pieces)
    for offset, column, count in items:
        at = grid_place(offset, factors, axis)
        mine = lax.rem(lax.axis_index(axis), count) if count > 1 else 0
        depth, width = pieces[0].shape
        columns = slice(column, column + width)
        start = pl.multiple_of(at * (count * depth), 16)
        for i in range(count):
            row = start + lax.rem(mine + i, count) * depth
            weight[pl.ds(pl.multiple_of(row, 16), depth), columns] = pieces.pop(0)[...]
        value = weight[pl.ds(start, count * depth), columns]
        total[:, columns] += dot(jnp.concatenate([cut_f[at], cut_b[at]], axis=0), value)


def flat(group):
    return [p for item in group for p in item[0]], [(o, c, len(p)) for p, o, c in group]


def keyval_kernel(items, count, factors, axis, first, *refs):
    cut_f, cut_b = refs[:2]
    pieces, (total, weight) = refs[2 : 2 + count], refs[-2:]
    total[...] = jnp.zeros_like(total) if first else refs[2 + count][...]
    add_pieces(items, factors, axis, cut_f, cut_b, pieces, total, weight)


def keyval_call(cut_f, cut_b, group, factors, axis, state, shape):
    pieces, items = flat(group)
    rows = 2 * cut_f.shape[1]
    work = rows * sum(p.size for p in pieces)
    n = 2 + len(pieces)
    return pl.pallas_call(
        functools.partial(keyval_kernel, items, len(pieces), factors, axis, state is None),
        out_shape=(
            jax.ShapeDtypeStruct((rows, shape[1]), F32),
            jax.ShapeDtypeStruct(shape, BF16),
        ),
        input_output_aliases={} if state is None else {n: 0, n + 1: 1},
        cost_estimate=pl.CostEstimate(
            flops=2 * work, bytes_accessed=work // rows * 2, transcendentals=0
        ),
        compiler_params=pltpu.CompilerParams(vmem_limit_bytes=12 << 20),
        name="keyval",
    )(cut_f, cut_b, *pieces, *(() if state is None else state))


def beside(x):
    _, width = x.shape
    wide = jnp.concatenate([x] * SIDE, axis=1)
    lane = lax.broadcasted_iota(jnp.int32, wide.shape, 1)
    blocks = [
        jnp.where((lane >= j * width) & (lane < (j + 1) * width), wide, jnp.zeros_like(wide))
        for j in range(SIDE)
    ]
    return jnp.concatenate(blocks, axis=0)


def diagonal(x, rows, width):
    total = x[:rows, :width]
    for j in range(1, SIDE):
        total = total + x[j * rows : (j + 1) * rows, j * width : (j + 1) * width]
    return total


def same_segment(rows):
    size = SIDE * rows
    a = lax.broadcasted_iota(jnp.int32, (size, size), 0) // rows
    b = lax.broadcasted_iota(jnp.int32, (size, size), 1) // rows
    return (a == b).astype(F32).astype(BF16)


def segment_sum(x, ones):
    high = x.astype(BF16)
    low = (x - high.astype(F32)).astype(BF16)
    return dot(high, ones) + dot(low, ones)


def segment_max(x, rows):
    tiles = []
    for start in range(0, x.shape[1], 128):
        tile = x[:, start : start + 128]
        lane = lax.broadcasted_iota(jnp.int32, tile.shape, 1)
        top = None
        for low in range(0, 128, rows):
            inside = (lane >= low) & (lane < low + rows)
            part = jnp.max(jnp.where(inside, tile, -3e38), axis=-1, keepdims=True)
            top = jnp.broadcast_to(part, tile.shape) if top is None else jnp.where(lane >= low, part, top)
        tiles.append(top)
    return jnp.concatenate(tiles, axis=1)


def staggered(stages, count):
    for step in range(count + len(stages) - 1):
        for i, stage in enumerate(stages):
            if 0 <= step - i < count:
                stage(step - i)


def allowed_mask(docs_ref):
    rows = docs_ref.shape[1]
    row = lax.broadcasted_iota(jnp.int32, (rows, rows), 0)
    col = lax.broadcasted_iota(jnp.int32, (rows, rows), 1)
    across = jnp.broadcast_to(docs_ref[...].astype(F32), (rows, rows))
    down = jnp.sum(jnp.where(row == col, across, 0.0), axis=1, keepdims=True)
    allowed = jnp.where((across == down) & (col <= row), 1.0, 0.0)
    allowed = jnp.concatenate([allowed] * SIDE, axis=1)
    return jnp.concatenate([allowed] * (GROUP // SIDE), axis=0) > 0.5


def stacked(ref, k):
    wide = SIDE * HD
    groups = GROUP // SIDE
    return jnp.concatenate(
        [ref[:, (k * groups + g) * wide : (k * groups + g + 1) * wide] for g in range(groups)], axis=0
    )


def place_columns(ref, at, depth, value):
    if depth % 128 == 0:
        ref[:, pl.ds(pl.multiple_of(at * depth, 128), depth)] = value
        return
    span = pl.ds(pl.multiple_of(lax.div(at, 2) * (2 * depth), 128), 2 * depth)
    old = ref[:, span]
    low = jnp.concatenate([value, old[:, depth:]], axis=1)
    high = jnp.concatenate([old[:, :depth], value], axis=1)
    ref[:, span] = jnp.where(lax.rem(at, 2) == 1, high, low)


def turn_kernel(items, count, factors, axis, *refs):
    cut_f, cut_b = refs[:2]
    pieces, refs = refs[2 : 2 + count], refs[2 + count :]
    old, _, total, weight, turned = refs
    total[...] = old[...]
    add_pieces(items, factors, axis, cut_f, cut_b, pieces, total, weight)
    step = weight.shape[0] // 9
    for c in range(0, weight.shape[0], step):
        turned[:, c : c + step] = weight[c : c + step, :].T


def turn_pieces(items, count, factors, axis, weight, turned):
    for offset, column, pair in items:
        at = grid_place(offset, factors, axis)
        depth = weight.shape[0] // count
        columns = slice(column, column + KVH * HD)
        value = weight[pl.ds(pl.multiple_of(at * depth, 16), depth), columns]
        place_columns(turned.at[columns, :], at, depth, value.T)


def turn_call(cut_f, cut_b, group, factors, axis, state):
    pieces, items = flat(group)
    n = 2 + len(pieces)
    shape = state[1].shape
    return pl.pallas_call(
        functools.partial(turn_kernel, items, len(pieces), factors, axis),
        out_shape=(
            jax.ShapeDtypeStruct(state[0].shape, F32),
            jax.ShapeDtypeStruct(shape, BF16),
            jax.ShapeDtypeStruct(shape[::-1], BF16),
        ),
        input_output_aliases={n: 0, n + 1: 1},
        cost_estimate=pl.CostEstimate(
            flops=1 << 27, bytes_accessed=2 * shape[0] * shape[1], transcendentals=0
        ),
        compiler_params=pltpu.CompilerParams(vmem_limit_bytes=12 << 20),
        name="turn",
    )(cut_f, cut_b, *pieces, *state)


def probs_kernel(items, count, factors, axis, *refs):
    cut_f, cut_b = refs[:2]
    pieces, refs = refs[2 : 2 + count], refs[2 + count :]
    (old, _, _, hid_f, hid_b, docs_f, docs_b,
     total, weight, turned, probs_f, probs_b, key_b) = refs
    rows = hid_f.shape[0]
    total[...] = old[...]
    add_pieces(items, factors, axis, cut_f, cut_b, pieces, total, weight)
    turn_pieces(items, cut_f.shape[0], factors, axis, weight, turned)
    keys = total[:, : KVH * HD].astype(BF16)
    across = keys.T
    ones = same_segment(rows)
    masks = (allowed_mask(docs_f), allowed_mask(docs_b))
    held = {}

    def score(n):
        k, back = n // 2, 1 - n % 2
        key = beside(across[k * HD : (k + 1) * HD, back * rows : (back + 1) * rows])
        held[n] = dot(stacked((hid_f, hid_b)[back], k), key) * HD**-0.5
        if back:
            key_b[k] = beside(keys[rows:, k * HD : (k + 1) * HD])

    def power(n):
        scores = jnp.where(masks[1 - n % 2], held[n], -1e30)
        held[n] = jnp.exp(scores - segment_max(scores, rows))

    def divide(n):
        powers = held.pop(n)
        probs = powers * (1.0 / segment_sum(powers, ones))
        if n % 2 == 0:
            probs_b[n // 2] = probs
        else:
            probs_f[n // 2] = probs.astype(BF16)

    staggered((score, power, divide), 2 * KVH)


def probs_call(cut_f, cut_b, group, factors, axis, state, turned, hid_f, hid_b, docs):
    pieces, items = flat(group)
    rows = hid_f.shape[0]
    n = 2 + len(pieces)
    scores = (KVH, GROUP // SIDE * rows, SIDE * rows)
    return pl.pallas_call(
        functools.partial(probs_kernel, items, len(pieces), factors, axis),
        out_shape=(
            jax.ShapeDtypeStruct(state[0].shape, F32),
            jax.ShapeDtypeStruct(state[1].shape, BF16),
            jax.ShapeDtypeStruct(turned.shape, BF16),
            jax.ShapeDtypeStruct(scores, BF16),
            jax.ShapeDtypeStruct(scores, F32),
            jax.ShapeDtypeStruct((KVH, SIDE * rows, SIDE * HD), BF16),
        ),
        input_output_aliases={n: 0, n + 1: 1, n + 2: 2},
        cost_estimate=pl.CostEstimate(flops=1 << 28, bytes_accessed=1 << 22, transcendentals=1 << 19),
        compiler_params=pltpu.CompilerParams(vmem_limit_bytes=12 << 20),
        name="probs",
    )(cut_f, cut_b, *pieces, *state, turned, hid_f, hid_b, *docs)


def more_kernel(items, count, factors, axis, *refs):
    cut_f, cut_b = refs[:2]
    pieces, refs = refs[2 : 2 + count], refs[2 + count :]
    old, _, _, total, weight, turned = refs
    total[...] = old[...]
    add_pieces(items, factors, axis, cut_f, cut_b, pieces, total, weight)
    turn_pieces(items, cut_f.shape[0], factors, axis, weight, turned)


def more_call(cut_f, cut_b, group, factors, axis, state, turned):
    pieces, items = flat(group)
    n = 2 + len(pieces)
    return pl.pallas_call(
        functools.partial(more_kernel, items, len(pieces), factors, axis),
        out_shape=(
            jax.ShapeDtypeStruct(state[0].shape, F32),
            jax.ShapeDtypeStruct(state[1].shape, BF16),
            jax.ShapeDtypeStruct(turned.shape, BF16),
        ),
        input_output_aliases={n: 0, n + 1: 1, n + 2: 2},
        cost_estimate=pl.CostEstimate(flops=1 << 26, bytes_accessed=1 << 20, transcendentals=0),
        compiler_params=pltpu.CompilerParams(vmem_limit_bytes=12 << 20),
        name="more",
    )(cut_f, cut_b, *pieces, *state, turned)


def mid_kernel(turned, probs_b, cot_ref, grad_v, through):
    rows, depth = through.shape
    keys = KVH * HD
    step = depth // 9
    for k in range(KVH):
        grad = dot(probs_b[k].astype(BF16), stacked(cot_ref, k), ((0,), (0,)))
        grad_v[:, k * HD : (k + 1) * HD] = diagonal(grad, rows, HD).astype(BF16)
    grads = grad_v[...]
    for c in range(0, depth, step):
        at = slice(c, c + step)
        through[:, at] = dot(grads, turned[keys:, at])


def mid_call(turned, probs_b, cotangent):
    rows, width = cotangent.shape
    return pl.pallas_call(
        mid_kernel,
        out_shape=(
            jax.ShapeDtypeStruct((rows, KVH * HD), BF16),
            jax.ShapeDtypeStruct((rows, width), F32),
        ),
        cost_estimate=pl.CostEstimate(flops=1 << 28, bytes_accessed=1 << 22, transcendentals=0),
        compiler_params=pltpu.CompilerParams(vmem_limit_bytes=12 << 20),
        name="mid",
    )(turned, probs_b, cotangent)


def last_values(items, factors, axis, cut_f, cut_b, pieces, grad_v):
    pieces, total, late = list(pieces), 0.0, []
    for offset, column, count in items:
        at = grid_place(offset, factors, axis)
        depth = pieces[0].shape[0]
        left = jnp.concatenate([cut_f[at], cut_b[at]], axis=0)
        values = [pieces.pop(0)[...] for _ in range(count)]
        lefts = [left[:, i * depth : (i + 1) * depth] for i in range(count)]
        parts = [dot(grad_v, value.T) for value in values]
        if count == 2:
            second = lax.rem(lax.axis_index(axis), 2) == 1
            lefts = [jnp.where(second, lefts[1 - i], lefts[i]) for i in range(2)]
            parts = [jnp.where(second, parts[1 - i], parts[i]) for i in range(2)]
        for mine, value in zip(lefts, values):
            total = total + dot(mine, value)
        late.append((at, count * depth, jnp.concatenate(parts, axis=1)))
    return total, late


def tail_kernel(items, count, factors, axis, *refs):
    cut_f, cut_b = refs[:2]
    pieces, refs = refs[2 : 2 + count], refs[2 + count :]
    (total_ref, half_ref, probs_f, probs_b, key_b, grad_v, turned, queries, u_ref, saved_ref,
     cot_ref, scale_ref, gain_scale, gain_values), refs = refs[:14], refs[14:]
    fwd_out, back_out, through, fwd_ref, back_ref, grad_q, grad_k, sems = refs
    rows, width = u_ref.shape
    keys = KVH * HD
    groups = GROUP // SIDE
    wide = SIDE * HD
    copies = []

    def send(source, target, at):
        copies.append(pltpu.make_async_copy(source.at[at], target.at[at], sems.at[len(copies)]))
        copies[-1].start()

    total, late = last_values(items, factors, axis, cut_f, cut_b, pieces, grad_v[...])
    total = total_ref[:, keys:] + total
    for at, depth, value in late:
        place_columns(through, at, depth, value)
    values = total.astype(BF16)
    across = values[rows:].T
    ones = same_segment(rows)
    held = {}

    def grad_probs(k):
        value = beside(across[k * HD : (k + 1) * HD])
        held[k] = dot(stacked(cot_ref, k), value).astype(BF16).astype(F32)

    def grad_scores(k):
        probs = probs_b[k]
        mean = dot((probs * held[k]).astype(BF16), ones)
        held[k] = (probs * (held[k] - mean) * HD**-0.5).astype(BF16)

    def grad_inputs(k):
        scores = held.pop(k)
        grad_queries = dot(scores, key_b[k]).astype(BF16)
        for g in range(groups):
            at = (k * groups + g) * wide
            grad_q[:, at : at + wide] = grad_queries[g * rows : (g + 1) * rows]
        grad = dot(queries[k], scores)
        part = grad[:HD, :rows]
        for j in range(1, SIDE):
            part = part + grad[j * HD : (j + 1) * HD, j * rows : (j + 1) * rows]
        grad_k[k * HD : (k + 1) * HD, :] = part

    def forward(k):
        mixed = dot(probs_f[k], beside(values[:rows, k * HD : (k + 1) * HD]))
        for g in range(groups):
            at = (k * groups + g) * wide
            fwd_ref[:, at : at + wide] = (
                u_ref[:, at : at + wide].astype(F32) + mixed[g * rows : (g + 1) * rows]
            ).astype(BF16)
        if k == KVH - 1:
            send(fwd_ref, fwd_out, slice(0, rows))

    staggered((forward, grad_probs, grad_scores, grad_inputs), KVH)
    grads = grad_k[...].T.astype(BF16)
    step = width // 9
    along = jnp.zeros((rows, 1), F32)
    for c in range(0, width, step):
        at = slice(c, c + step)
        full = dot(grads, turned[:keys, at]) + through[:, at] + grad_q[:, at].astype(F32)
        full = full.astype(BF16).astype(F32)
        through[:, at] = full
        along = along + jnp.sum(full * gain_values[:, at], axis=-1, keepdims=True)
    scale = scale_ref[:, :1]
    along = along * (scale * scale * scale) / width
    block = rows // BLOCKS
    for low in range(0, rows, block):
        lines = slice(low, low + block)
        for c in range(0, width, step):
            at = (lines, slice(c, c + step))
            grad = through[at] * gain_scale[at] - saved_ref[at].astype(F32) * along[lines]
            back_ref[at] = cot_ref[at] + grad.astype(BF16)
        send(back_ref, back_out, lines)
    for copy in copies:
        copy.wait()


def tail_call(cut_f, cut_b, group, factors, axis, total, through, *others):
    pieces, items = flat(group)
    rows, width = through.shape
    vmem, hbm = pl.BlockSpec(memory_space=pltpu.VMEM), pl.BlockSpec(memory_space=pl.ANY)
    operands = (cut_f, cut_b, *pieces, total, through, *others)
    fwd_out, back_out, _ = pl.pallas_call(
        functools.partial(tail_kernel, items, len(pieces), factors, axis),
        out_shape=(
            jax.ShapeDtypeStruct((rows, width), BF16),
            jax.ShapeDtypeStruct((rows, width), BF16),
            jax.ShapeDtypeStruct(through.shape, F32),
        ),
        in_specs=[vmem] * len(operands),
        out_specs=(hbm, hbm, vmem),
        input_output_aliases={3 + len(pieces): 2},
        scratch_shapes=[
            pltpu.VMEM((rows, width), BF16),
            pltpu.VMEM((rows, width), BF16),
            pltpu.VMEM((rows, width), BF16),
            pltpu.VMEM((KVH * HD, rows), F32),
            pltpu.SemaphoreType.DMA((1 + BLOCKS,)),
        ],
        cost_estimate=pl.CostEstimate(flops=1 << 29, bytes_accessed=1 << 23, transcendentals=0),
        compiler_params=pltpu.CompilerParams(vmem_limit_bytes=12 << 20),
        name="tail",
    )(*operands)
    return fwd_out, back_out


def shifted(x, axis, factors, steps):
    n = lax.axis_size(axis)
    pairs = []
    for me in range(n):
        source, stride = 0, 1
        for size, step in zip(reversed(factors), reversed(steps)):
            source = source + (me // stride % size + step) % size * stride
            stride = stride * size
        pairs.append((source, me))
    return lax.ppermute(x, axis, pairs)


def grid_factors(mesh, axis):
    n = mesh.shape[axis]
    place = list(mesh.axis_names).index(axis)
    devices = mesh.devices
    line = devices[tuple(slice(None) if i == place else 0 for i in range(devices.ndim))]
    spots = [(*getattr(d, "coords", (i,)), getattr(d, "core_on_chip", 0)) for i, d in enumerate(line)]
    factors, stride = [], 1
    while stride < n:
        moved = [i for i in range(len(spots[0])) if spots[stride][i] != spots[0][i]][0]
        size = len({s[moved] for s in spots[::stride]})
        factors.insert(0, size)
        stride *= size
    return tuple(factors)


def on_device(factors, fwd_prev, saved, back_prev, fwd_docs, back_docs, gain, weight):
    sections = lax.axis_size("section")
    own = weight[0]
    ring = lambda x, by: lax.ppermute(x, "section", [(i, (i + by) % sections) for i in range(sections)])

    def move(x, *steps):
        return shifted(x, "fsdp", factors, steps)

    half = own.shape[1] // 2
    keys = lambda x: x[:, :half]
    values = lambda x: x[:, half:]
    if relayed(factors):
        y0 = move(own, 0, 1, 0)
        z1 = move(own, 1, 0, 0)
        own_k, own_v = keys(own), values(own)
        z3k = move(own_k, 3, 0, 0)
        incoming = ring(fwd_prev[0], 1)
        cotangent = ring(back_prev[0], -1)
        c0 = move(own, 0, 0, 1)
        y1 = move(z1, 0, 1, 0)
        z2k = move(keys(z1), 1, 0, 0)
        z2v = move(values(z1), 1, 0, 0)
        z3v = move(own_v, 3, 0, 0)
        z3yv = move(values(y0), 3, 0, 0)
        y3k = move(z3k, 0, 1, 0)
        y2k = move(z2k, 0, 1, 0)
        y2v = move(z2v, 0, 1, 0)

        def both(x, z, y, column=0):
            return ([x, move(x, 0, 0, 1)], (z, y), column)

        groups = [
            ("keyval", [([own, c0], (0, 0), 0), both(y0, 0, 1), both(z1, 1, 0)]),
            ("keyval", [both(z3k, 3, 0), both(y1, 1, 1), both(z2k, 2, 0)]),
            ("turn", [both(z2v, 2, 0, half), both(y3k, 3, 1)]),
            ("more", [both(z3v, 3, 0, half)]),
            ("probs", [both(y2k, 2, 1)]),
            ("tail", [both(z3yv, 3, 1, half), both(y2v, 2, 1, half)]),
        ]
        parts, grid, axis = factors[0] * factors[1], factors, "fsdp"
    else:
        incoming = ring(fwd_prev[0], 1)
        cotangent = ring(back_prev[0], -1)
        full = lax.all_gather(own, "fsdp", axis=0, tiled=True)
        first, second, third, fourth = jnp.split(full, 4)
        groups = [
            ("keyval", [([first], (0,), 0), ([second], (1,), 0)]),
            ("turn", [([keys(third)], (2,), 0)]),
            ("more", [([values(third)], (2,), half)]),
            ("probs", [([keys(fourth)], (3,), 0)]),
            ("tail", [([values(fourth)], (3,), half)]),
        ]
        parts, grid, axis = 4, (4,), None
    hid_b, cut_b, scale_b, gain_scale, gain_values, turned_b = norm_call(saved[0], gain, parts, True)
    hid_f, cut_f = norm_call(incoming, gain, parts, False)
    state, turned = None, None
    for kind, group in groups[:-1]:
        if kind == "turn":
            *state, turned = turn_call(cut_f, cut_b, group, grid, axis, state)
        elif kind == "probs":
            *state, turned, probs_f, probs_b, key_b = probs_call(
                cut_f, cut_b, group, grid, axis, state, turned, hid_f, hid_b,
                (fwd_docs, back_docs),
            )
        elif kind == "more":
            *state, turned = more_call(cut_f, cut_b, group, grid, axis, state, turned)
        else:
            state = keyval_call(
                cut_f, cut_b, group, grid, axis, state, (saved.shape[2], own.shape[1])
            )
    grad_v, through = mid_call(turned, probs_b, cotangent)
    fwd_out, back_out = tail_call(
        cut_f, cut_b, groups[-1][1], grid, axis, state[0], through, probs_f, probs_b, key_b,
        grad_v, turned, turned_b, incoming, saved[0], cotangent, scale_b, gain_scale, gain_values,
    )
    return (fwd_out[None], back_out[None])


def relayed(factors):
    return len(factors) == 3 and factors[0] == 4 and factors[1:] == (2, 2)


def solution(mesh):
    in_specs = (
        P("section", "fsdp", None),
        P("section", "fsdp", None),
        P("section", "fsdp", None),
        P("section", "fsdp"),
        P("section", "fsdp"),
        P("section", None),
        P("section", "fsdp", None),
    )
    out_specs = (P("section", "fsdp", None), P("section", "fsdp", None))
    factors = grid_factors(mesh, "fsdp")
    return jax.shard_map(
        functools.partial(on_device, factors),
        mesh=mesh, in_specs=in_specs, out_specs=out_specs, check_vma=False,
    )
```
